1024 devices in a mesh: lat: 16 (over z, core), lon: 64 (over y, x).
Axes of the slice: x: 8, y: 8, z: 8, core: 2. Of those that a mesh axis runs over, the one named last changes fastest.
Arguments:
- field: bfloat16 [16, 10616832], P(None, ('lat', 'lon')), may hold values from -6 to 6
- dep_frac: float32 [10616832], P(('lat', 'lon')), may hold values from 0 to 1
- dep_index: int32 [2, 10616832], P(None, ('lat', 'lon')), may hold values from 0 to 11663, as said below
- send_list: int32 [1024, 2, 8], P(('lat', 'lon')), may hold values from 0 to 128, as said below
- send_count: int32 [1024, 2], P(('lat', 'lon')), may hold values from 0 to 8, as said below
- cycle_len: int32 [16, 128], P('lat'), may hold values from 20 to 5136, as said below
- diffusion: float32 [16], replicated, may hold values from 0.1 to 10
Outputs:
- smoothed: bfloat16 [16, 10616832], P(None, ('lat', 'lon'))
The draws below stay inside these ranges and needn't reach their ends.
Inputs may be any that keep to these rules, and one draw needn't show every extreme that they name: `cycle_len`: every circle length is 4 j + 16 for a whole number j. `send_count`: counts of used list entries; some device uses all 8. `send_list`: the used entries of a list are distinct circle numbers below 128; every unused entry is 128. `dep_index`: positions in the column's own device's extended list of 11664 columns; row 1 is row 0 plus one.
All inputs are finite; a program needn't handle non-finite values.
Results may differ from the reference program's by a relative error of at most 0.0049.
Values may be sent and summed in bfloat16 or wider, within the bound.
No kernel may reach another device: no remote copies, remote signals or barrier semaphores. Data moves between devices by JAX's collectives and lax.ppermute only.
A program may use at most 32 MiB of HBM per device.

```python
import math
import jax
import jax.numpy as jnp
from jax import lax

LMAX = 5136
TRUNC = 640
HALO_BLOCKS = 8
CH = 16
CYCLES = 128
SLOTS = 81
OWN = 10368
COLS = 10616832
N_LAT = 16
N_LON = 64


def halo_counts(key):
    base_key = jax.random.fold_in(key, 11)
    count_key, spot_key = jax.random.split(base_key)
    total_rows = N_LAT * N_LON * 2
    flat_counts = jax.random.randint(count_key, (total_rows,), 0, HALO_BLOCKS + 1)
    full_spot = jax.random.randint(spot_key, (), 0, total_rows)
    flat_counts = jnp.where(jnp.arange(total_rows) == full_spot, HALO_BLOCKS, flat_counts)
    return flat_counts.reshape(N_LAT * N_LON, 2).astype(jnp.int32)


def draw_send_count(key, part):
    return halo_counts(key)


def draw_send_list(key, part):
    counts = halo_counts(key)
    score_key = jax.random.fold_in(key, 12)
    scores = jax.random.randint(score_key, (N_LAT * N_LON, 2, CYCLES), 0, 1 << 20)
    scores = scores * CYCLES + jnp.arange(CYCLES, dtype=jnp.int32)[None, None, :]
    sorted_ids = jnp.argsort(scores, axis=2)[:, :, :HALO_BLOCKS]
    used_mask = jnp.arange(HALO_BLOCKS)[None, None, :] < counts[:, :, None]
    return jnp.where(used_mask, sorted_ids, CYCLES).astype(jnp.int32)


def draw_cycle_len(key, part):
    base_key = jax.random.fold_in(key, 13)
    cycle_key, first_key, second_random_key = jax.random.split(base_key, 3)
    top_cycle = (LMAX - 16) // 4
    total_cycles = N_LAT * CYCLES
    cycle_rows = jax.random.randint(cycle_key, (total_cycles,), 1, top_cycle + 1)
    first_spot = jax.random.randint(first_key, (), 0, total_cycles)
    second_spot = (first_spot + 1 + jax.random.randint(second_random_key, (), 0, total_cycles - 1)) % total_cycles
    positions = jnp.arange(total_cycles)
    cycle_rows = jnp.where(positions == first_spot, 1, cycle_rows)
    cycle_rows = jnp.where(positions == second_spot, top_cycle, cycle_rows)
    return (4 * cycle_rows + 16).reshape(N_LAT, CYCLES).astype(jnp.int32)


def draw_dep_index(key, part):
    base_key = jax.random.fold_in(key, 14)
    shift_key, far_key, pick_key, spot_key, other_key = jax.random.split(base_key, 5)
    own_cols = CYCLES * SLOTS
    extent_cols = own_cols + 2 * HALO_BLOCKS * SLOTS
    column = jnp.arange(COLS, dtype=jnp.int32) % own_cols
    shifts = jax.random.randint(shift_key, (COLS,), -2, 3)
    near_value = jnp.clip(column + shifts, 0, own_cols - 2)
    far_value = own_cols + jax.random.randint(far_key, (COLS,), 0, 2 * HALO_BLOCKS * SLOTS - 1)
    picked = jax.random.randint(pick_key, (COLS,), 0, 4) == 0
    lower_value = jnp.where(picked, far_value, near_value)
    first_spot = jax.random.randint(spot_key, (), 0, COLS)
    second_spot = (first_spot + 1 + jax.random.randint(other_key, (), 0, COLS - 1)) % COLS
    positions = jnp.arange(COLS)
    lower_value = jnp.where(positions == first_spot, 0, lower_value)
    lower_value = jnp.where(positions == second_spot, extent_cols - 2, lower_value)
    return jnp.stack([lower_value, lower_value + 1]).astype(jnp.int32)


def block_levels(rng, extent, pieces, low, top_value):
    gain = 1.0
    for dim, blocks in pieces:
        heights = jax.random.uniform(jax.random.fold_in(jax.random.fold_in(rng, 6), dim), (blocks,), jnp.float32, low / len(pieces), top_value / len(pieces))
        gain = gain * jnp.repeat(jnp.exp(heights), extent[dim] // blocks).reshape((-1,) + (1,) * (len(extent) - 1 - dim))
    return gain


def gaussian(rng, extent, scale, limit, pieces=(), kind=jnp.bfloat16):
    gain = block_levels(rng, extent, pieces, -0.22, 0.18) if pieces else 1.0
    entries = jax.random.normal(rng, extent, jnp.float32) * scale * gain
    return jnp.minimum(jnp.maximum(entries, -limit), limit).astype(kind)


def setup_inputs(seed: int = 0) -> dict:
    seeds = jax.random.split(jax.random.key(seed), 8)
    return {
        "field": gaussian(seeds[0], (CH, COLS), 1.0, 6.0, ((1, 1024),)),
        "dep_frac": jnp.clip(1.0 * jax.random.uniform(seeds[1], (COLS,), jnp.float32) ** block_levels(seeds[1], (COLS,), ((0, 1024),), -0.2, 0.2), 0.0, 1.0),
        "dep_index": draw_dep_index(jax.random.fold_in(seeds[7], 71), 0),
        "send_list": draw_send_list(jax.random.fold_in(seeds[7], 71), 0),
        "send_count": draw_send_count(jax.random.fold_in(seeds[7], 71), 0),
        "cycle_len": draw_cycle_len(jax.random.fold_in(seeds[7], 71), 0),
        "diffusion": jnp.clip(jnp.exp(jax.random.uniform(seeds[6], (CH,), jnp.float32, math.log(0.1), math.log(10.0))), 0.1, 10.0),
    }


def spectral_weights(wavenumber_index, length, length_real, diffusion):
    ratio = wavenumber_index.astype(jnp.float32) / TRUNC
    weight = jnp.where((wavenumber_index == 0) | (2 * wavenumber_index == length), 1.0, 2.0)
    weight = jnp.where(2 * wavenumber_index <= length, weight, 0.0)
    return weight[None, :] / ((1.0 + diffusion[:, None] * ratio[None, :] * ratio[None, :]) * length_real)


def filter_cycle(cycle_data, length, diffusion):
    channels, point_count = cycle_data.shape
    width = min(128, TRUNC)
    field_values = cycle_data.astype(jnp.float32)
    length_real = length.astype(jnp.float32)
    angle_scale = 2.0 * math.pi / length_real
    position = jnp.arange(point_count, dtype=jnp.int32)
    needed = (jnp.minimum(TRUNC, length // 2 + 1) + width - 1) // width

    def one_block(number, summed):
        wavenumber_index = number * width + jnp.arange(width, dtype=jnp.int32)
        phase = (position[:, None] * wavenumber_index[None, :]) % length
        angle = phase.astype(jnp.float32) * angle_scale
        table = jnp.concatenate([jnp.cos(angle), jnp.sin(angle)], axis=1)
        coeffs = jnp.dot(field_values, table, precision=lax.Precision.HIGHEST)
        damping = spectral_weights(wavenumber_index, length, length_real, diffusion)
        scaled = coeffs * jnp.concatenate([damping, damping], axis=1)
        return summed + jnp.dot(scaled, table.T, precision=lax.Precision.HIGHEST)

    summed = lax.fori_loop(0, needed, one_block, jnp.zeros((channels, point_count), jnp.float32))
    return jnp.where(position[None, :] < length, summed, 0.0).astype(jnp.bfloat16)


def reference(field, dep_frac, dep_index, send_list, send_count, cycle_len, diffusion):
    grid = field.astype(jnp.float32).reshape(CH, N_LAT, N_LON, CYCLES, SLOTS)
    slot_ids = jnp.arange(SLOTS, dtype=jnp.int32)
    lon_ids = jnp.arange(N_LON, dtype=jnp.int32)
    cycle_point = slot_ids[None, :] * N_LON + lon_ids[:, None]
    validity_mask = cycle_point[None, :, None, :] < cycle_len[:, None, :, None]
    masked = jnp.where(validity_mask[None], grid, 0.0)
    lists = send_list.reshape(N_LAT, N_LON, 2, HALO_BLOCKS)
    counts = send_count.reshape(N_LAT, N_LON, 2)
    kept_mask = jnp.arange(HALO_BLOCKS, dtype=jnp.int32)[None, None, None, :] < counts[:, :, :, None]
    band_ids = jnp.arange(N_LAT, dtype=jnp.int32)[:, None, None, None]
    set_ids = lon_ids[None, :, None, None]
    picked = masked[:, band_ids, set_ids, jnp.clip(lists, 0, CYCLES - 1), :]
    picked = jnp.where(kept_mask[None, :, :, :, :, None], picked, 0.0)
    zeros_band = jnp.zeros_like(picked[:, :1, :, 0])
    from_north = jnp.concatenate([zeros_band, picked[:, :-1, :, 1]], axis=1)
    from_south = jnp.concatenate([picked[:, 1:, :, 0], zeros_band], axis=1)
    extended = jnp.concatenate([masked.reshape(CH, N_LAT, N_LON, OWN),
                                from_north.reshape(CH, N_LAT, N_LON, HALO_BLOCKS * SLOTS),
                                from_south.reshape(CH, N_LAT, N_LON, HALO_BLOCKS * SLOTS)], axis=3)
    stencil = dep_index.reshape(2, N_LAT, N_LON, OWN)
    weights = dep_frac.reshape(N_LAT, N_LON, OWN)[None]
    lower_value = jnp.take_along_axis(extended, jnp.broadcast_to(stencil[0][None], (CH, N_LAT, N_LON, OWN)), axis=3)
    upper_value = jnp.take_along_axis(extended, jnp.broadcast_to(stencil[1][None], (CH, N_LAT, N_LON, OWN)), axis=3)
    blended = (1.0 - weights) * lower_value + weights * upper_value
    departed = jnp.where(validity_mask.reshape(1, N_LAT, N_LON, OWN), blended, 0.0).astype(jnp.bfloat16)
    cycle_major = departed.reshape(CH, N_LAT, N_LON, CYCLES, SLOTS).transpose(1, 3, 0, 4, 2)
    cycle_major = cycle_major.reshape(N_LAT * CYCLES, CH, SLOTS * N_LON)

    def apply_cycle(cycle_item):
        return filter_cycle(cycle_item[0], cycle_item[1], diffusion)

    filtered = lax.map(apply_cycle, (cycle_major, cycle_len.reshape(-1)))
    restored = filtered.reshape(N_LAT, CYCLES, CH, SLOTS, N_LON).transpose(2, 0, 4, 1, 3)
    return restored.reshape(CH, COLS)
```

```python
import math

import jax
import jax.numpy as jnp
from jax import lax
from jax.experimental import pallas as pl
from jax.experimental.pallas import tpu as pltpu
from jax.sharding import PartitionSpec as P

TRUNC = 640
HALO_BLOCKS = 8
CH = 16
CYCLES = 128
SLOTS = 81
N_LON = 64
OWN = CYCLES * SLOTS
HALO = HALO_BLOCKS * SLOTS
LANES = 128
STRIDE = 255
WINDOW = 256
EXT = OWN + 2 * HALO
N_WIN = (EXT - 2) // STRIDE + 1
HEAD = 64
TAIL = SLOTS - HEAD
SLOT_ROWS = 96
MAIN_COLS = N_LON * LANES
K_BLOCKS = TRUNC // LANES
OWN_WIN = OWN // STRIDE + 1
RIM_OWN = OWN - STRIDE * (OWN_WIN - 1)
RIM = -(-(STRIDE * (N_WIN - OWN_WIN) + WINDOW) // LANES) * LANES
BATCH = 2 * WINDOW
MAIN_STEPS = MAIN_COLS // BATCH
FULL_STEPS = OWN // BATCH
NEAR = 4
FAR = N_LON // NEAR
F32 = jnp.float32
BF16 = jnp.bfloat16


def lane_iota(rows, cols=LANES):
    return lax.broadcasted_iota(jnp.int32, (rows, cols), 1)


def slots_used(length, lon_index):
    return (length - lon_index + (N_LON - 1)) >> 6


def pick_kernel(list_ref, count_ref, len_ref, field_ref, first_ref, second_ref):
    lon_index = lax.axis_index("lon")
    lane = lane_iota(CH, 2 * LANES)
    for way, out_ref in ((0, first_ref), (1, second_ref)):
        blocks = [jnp.zeros((CH, LANES), F32) for _ in range(7)]
        for k in range(HALO_BLOCKS):
            row = jnp.clip(list_ref[0, way, k], 0, CYCLES - 1)
            start = row * SLOTS
            base = jnp.minimum(start >> 7, OWN // LANES - 2)
            shift = start - base * LANES
            place = (SLOTS * k) % LANES
            block = (SLOTS * k) // LANES
            window = field_ref[:, pl.ds(pl.multiple_of(base * LANES, LANES), 2 * LANES)]
            moved = pltpu.roll(window.astype(F32), (place - shift + 2 * LANES) & 255, 1)
            used = jnp.where(k < count_ref[0, way], slots_used(len_ref[0, row], lon_index), 0)
            keep = (lane >= place) & (lane < place + used)
            for half in range(2):
                part = slice(half * LANES, (half + 1) * LANES)
                blocks[block + half] = jnp.where(keep[:, part], moved[:, part], blocks[block + half])
        for i in range(5):
            out_ref[:, i * LANES : (i + 1) * LANES] = blocks[i].astype(BF16)
        out_ref[:, 5 * LANES : HALO] = blocks[5][:, : HALO - 5 * LANES].astype(BF16)


def prepare_kernel(len_ref, field_ref, index_ref, frac_ref, win_ref, where_ref, ext_ref, pair_ref):
    lon_index = lax.axis_index("lon")
    pair_ref[:, OWN:] = jnp.zeros((8, LANES), F32)
    pair_ref[0:1, 0:OWN] = index_ref[0:1, :].astype(F32)
    pair_ref[1:2, 0:OWN] = frac_ref[...]
    lane = lane_iota(8)
    tile = None
    for d in range(N_LON):
        used = [slots_used(len_ref[0, 2 * d + turn], lon_index) for turn in range(2)]
        begin = 2 * SLOTS * d
        here = jnp.where(
            lane < HEAD,
            pair_ref[:, begin : begin + LANES],
            pair_ref[:, begin + TAIL : begin + TAIL + LANES],
        )
        limit = jnp.where(lane < HEAD, used[0], used[1] + HEAD)
        here = jnp.where(lane < limit, here, -1.0)
        where_ref[:, LANES * d : LANES * (d + 1)] = here[0:2]
        for turn in range(2):
            at = TAIL * (2 * d + turn)
            number, place = at // LANES, at % LANES
            source = begin + SLOTS * turn + HEAD - place
            limit = place + used[turn] - HEAD
            here = jnp.where(lane < limit, pair_ref[:, source : source + LANES], -1.0)
            tile = here if tile is None else jnp.where(lane >= place, here, tile)
            if place + TAIL >= LANES:
                column = MAIN_COLS + LANES * number
                where_ref[:, column : column + LANES] = tile[0:2]
                tile = None
                if place + TAIL > LANES:
                    source += LANES
                    tile = jnp.where(lane < limit - LANES, pair_ref[:, source : source + LANES], -1.0)

    lane = lane_iota(CH)
    for b in range(OWN // LANES):
        first = (LANES * b) // SLOTS
        last = (LANES * b + LANES - 1) // SLOTS
        limit = SLOTS * last + slots_used(len_ref[0, last], lon_index) - LANES * b
        limit = jnp.full((CH, LANES), limit, jnp.int32)
        for r in range(last - 1, first - 1, -1):
            here = SLOTS * r + slots_used(len_ref[0, r], lon_index) - LANES * b
            limit = jnp.where(lane < SLOTS * (r + 1) - LANES * b, here, limit)
        keep = jnp.where(lane < limit, 1.0, 0.0).astype(BF16)
        part = slice(b * LANES, (b + 1) * LANES)
        ext_ref[:, part] = field_ref[:, part] * keep
    ext_ref[:, OWN : OWN + LANES] = jnp.zeros((CH, LANES), BF16)
    for q in range(OWN_WIN):
        win_ref[CH * q : CH * (q + 1), :] = ext_ref[:, STRIDE * q : STRIDE * q + WINDOW]


def gather_kernel(own_ref, north_ref, south_ref, where_ref, out_ref, rim_ref, win_ref, m0, m1, tail_ref):
    rim_ref[:, RIM_OWN + 2 * HALO :] = jnp.zeros((CH, RIM - RIM_OWN - 2 * HALO), BF16)
    rim_ref[:, 0:RIM_OWN] = own_ref[CH * (OWN_WIN - 1) : CH * OWN_WIN, 0:RIM_OWN]
    rim_ref[:, RIM_OWN : RIM_OWN + HALO] = north_ref[...]
    rim_ref[:, RIM_OWN + HALO : RIM_OWN + 2 * HALO] = south_ref[...]
    win_ref[0 : CH * (OWN_WIN - 1), :] = own_ref[0 : CH * (OWN_WIN - 1), :]
    for q in range(OWN_WIN - 1, N_WIN):
        at = STRIDE * (q - OWN_WIN + 1)
        win_ref[CH * q : CH * (q + 1), :] = rim_ref[:, at : at + WINDOW]

    def window_number(start, width):
        index = where_ref[0:1, pl.ds(start, width)].astype(jnp.int32)
        return index, (index * 32897) >> 23

    def make_weights(start, width, m_ref):
        index, number = window_number(start, width)
        frac = where_ref[1:2, pl.ds(start, width)]
        used = index >= 0
        offset = (index - STRIDE * number).astype(F32)
        offset = jnp.broadcast_to(offset, (16, width)).astype(BF16)
        low = jnp.broadcast_to(jnp.where(used, 1.0 - frac, 0.0), (16, width)).astype(BF16)
        high = jnp.broadcast_to(jnp.where(used, frac, 0.0), (16, width)).astype(BF16)
        row16 = lax.broadcasted_iota(jnp.int32, (16, width), 0).astype(F32)
        for s in range(WINDOW // 16):
            row = (row16 + 16.0 * s).astype(BF16)
            before = (row16 + (16.0 * s - 1.0)).astype(BF16)
            m_ref[16 * s : 16 * (s + 1), 0:width] = jnp.where(
                row == offset, low, jnp.where(before == offset, high, jnp.zeros_like(low))
            )

    def choose(start, width, m_ref):
        windows = jnp.dot(win_ref[...], m_ref[:, 0:width], preferred_element_type=F32)
        index, number = window_number(start, width)
        number = jnp.broadcast_to(number, (CH, width))
        bits = [(number & (1 << i)) != 0 for i in range(6)]

        def pick(low, level):
            if level == 0:
                return windows[CH * low : CH * (low + 1)]
            near = pick(low, level - 1)
            far = low + (1 << (level - 1))
            if far >= N_WIN:
                return near
            return jnp.where(bits[level - 1], pick(far, level - 1), near)

        return pick(0, 6)

    def put_main(step, m_ref):
        total = choose(pl.multiple_of(step * BATCH, BATCH), BATCH, m_ref).astype(BF16)
        for i in range(BATCH // LANES):
            out_ref[BATCH // LANES * step + i, 0:CH, :] = total[:, i * LANES : (i + 1) * LANES]

    def weights(step, m_ref):
        make_weights(pl.multiple_of(step * BATCH, BATCH), BATCH, m_ref)

    def main_pair(i, carry):
        weights(2 * i + 1, m1)
        put_main(2 * i, m0)
        weights(2 * i + 2, m0)
        put_main(2 * i + 1, m1)
        return carry

    def tail_pair(i, carry):
        step = MAIN_STEPS + 2 * i
        weights(step + 1, m1)
        at = pl.multiple_of(2 * i * BATCH, BATCH)
        tail_ref[:, pl.ds(at, BATCH)] = choose(pl.multiple_of(step * BATCH, BATCH), BATCH, m0)
        weights(jnp.minimum(step + 2, FULL_STEPS - 1), m0)
        step = step + 1
        at = pl.multiple_of(at + BATCH, BATCH)
        tail_ref[:, pl.ds(at, BATCH)] = choose(pl.multiple_of(step * BATCH, BATCH), BATCH, m1)
        return carry

    weights(0, m0)
    lax.fori_loop(0, MAIN_STEPS // 2, main_pair, 0)
    lax.fori_loop(0, (FULL_STEPS - MAIN_STEPS) // 2, tail_pair, 0)
    rest = FULL_STEPS * BATCH
    make_weights(rest, OWN - rest, m0)
    tail_ref[:, rest - MAIN_COLS :] = choose(rest, OWN - rest, m0)

    left = lane_iota(8) < 64
    for d in range(N_LON):
        at = 2 * TAIL * d
        tile, place = at // LANES, at % LANES
        halves = []
        for h in range(2):
            rows = slice(8 * h, 8 * h + 8)
            here = tail_ref[rows, tile * LANES : (tile + 1) * LANES]
            if place + 2 * TAIL > LANES:
                there = tail_ref[rows, (tile + 1) * LANES : (tile + 2) * LANES]
                here = jnp.where(lane_iota(8) >= place, here, there)
            halves.append(pltpu.roll(here, (64 * h - place) % LANES, 1))
        out_ref[d, CH : CH + 8, :] = jnp.where(left, halves[0], halves[1]).astype(BF16)


def cos_sin(product, length, inverse):
    turns = product - jnp.round(product * inverse) * length
    half = turns * (inverse * math.pi)
    z = half * half
    s = -1.0 / 39916800.0
    for c in (1.0 / 362880.0, -1.0 / 5040.0, 1.0 / 120.0, -1.0 / 6.0, 1.0):
        s = s * z + c
    s = s * half
    c0 = 1.0 / 479001600.0
    for c in (-1.0 / 3628800.0, 1.0 / 40320.0, -1.0 / 720.0, 1.0 / 24.0, -0.5, 1.0):
        c0 = c0 * z + c
    return 1.0 - 2.0 * s * s, 2.0 * s * c0


def rotate(cosine, sine, by_cos, by_sin):
    return cosine * by_cos - sine * by_sin, sine * by_cos + cosine * by_sin


def spectral_kernel(len_ref, diff_ref, in_ref, out_ref, x0, x1, w_ref, base_ref, p_ref, y_ref):
    lon_index = lax.axis_index("lon")
    lengths = [len_ref[0, 2 * lon_index + turn] for turn in range(2)]
    for near in range(NEAR):
        w_ref[LANES * near + SLOT_ROWS : LANES * (near + 1), :] = jnp.zeros(
            (LANES - SLOT_ROWS, 4 * TRUNC), BF16
        )
    left = lane_iota(8) < 64

    def load_step(far, carry):
        at = pl.multiple_of(far * CH, CH)
        for near in range(NEAR):
            l = far * NEAR + near
            main = in_ref[l, 0:CH, :].astype(F32)
            tail = in_ref[l, CH : CH + 8, :].astype(F32)
            swap = pltpu.roll(main, 64, 1)
            first = [
                jnp.where(left, main[0:8], pltpu.roll(tail, 64, 1)),
                jnp.where(left, main[8:16], tail),
            ]
            second = [
                jnp.where(left, swap[0:8], pltpu.roll(tail, HEAD - TAIL, 1)),
                jnp.where(left, swap[8:16], pltpu.roll(tail, LANES - TAIL, 1)),
            ]
            lanes = slice(LANES * near, LANES * (near + 1))
            x0[pl.ds(at, CH), lanes] = jnp.concatenate(first, axis=0).astype(BF16)
            x1[pl.ds(at, CH), lanes] = jnp.concatenate(second, axis=0).astype(BF16)
        return carry

    lax.fori_loop(0, FAR, load_step, 0, unroll=2)

    row = lax.broadcasted_iota(jnp.int32, (CH, LANES), 0)
    diffusion = jnp.zeros((CH, LANES), F32)
    for c in range(CH):
        diffusion = jnp.where(row == c, diff_ref[c], diffusion)

    first_row = lax.broadcasted_iota(jnp.int32, (8, LANES), 0) == 0
    i48 = lax.broadcasted_iota(jnp.int32, (48, LANES), 0)
    factor = jnp.where(
        i48 < 8,
        N_LON * i48,
        jnp.where(i48 < 24, 8 * N_LON * (i48 - 8), jnp.where(i48 < 40, NEAR * (i48 - 24), i48 - 40)),
    ).astype(F32)

    for turn in range(2):
        length_int = lengths[turn]
        x_ref = (x0, x1)[turn]

        def block_step(block, carry, turn=turn, length_int=length_int, x_ref=x_ref):
            length = jnp.full((1, LANES), length_int, jnp.int32).astype(F32)
            inverse = 1.0 / length
            wave = lane_iota(1) + block * LANES
            wave_f = wave.astype(F32)
            column = pl.multiple_of((turn * K_BLOCKS + block) * 2 * LANES, 2 * LANES)
            cosine, sine = cos_sin(factor * wave_f, length, inverse)
            base_ref[:, 0:LANES] = cosine
            base_ref[:, LANES : 2 * LANES] = sine

            def base(i):
                return base_ref[i : i + 1, 0:LANES], base_ref[i : i + 1, LANES : 2 * LANES]

            low_cos, low_sin = cosine[0:8], sine[0:8]
            for pair in range(SLOT_ROWS // 16):
                strips = [rotate(low_cos, low_sin, *base(8 + 2 * pair + h)) for h in range(2)]
                if pair == SLOT_ROWS // 16 - 1:
                    strips[0] = [jnp.where(first_row, v, 0.0) for v in strips[0]]
                    strips[1] = [jnp.zeros_like(v) for v in strips[1]]
                for near in range(NEAR):
                    turned = strips if near == 0 else [rotate(*st, *base(40 + near)) for st in strips]
                    both = jnp.concatenate(
                        [
                            jnp.concatenate([turned[0][0], turned[1][0]], axis=0),
                            jnp.concatenate([turned[0][1], turned[1][1]], axis=0),
                        ],
                        axis=1,
                    )
                    at = LANES * near + 16 * pair
                    w_ref[at : at + 16, pl.ds(column, 2 * LANES)] = both.astype(BF16)
            partial = jnp.dot(
                x_ref[...], w_ref[:, pl.ds(column, 2 * LANES)], preferred_element_type=F32
            )
            coeff_cos = jnp.zeros((CH, LANES), F32)
            coeff_sin = jnp.zeros((CH, LANES), F32)
            for far in range(FAR):
                here = partial[CH * far : CH * (far + 1)]
                far_cos, far_sin = base(24 + far)
                coeff_cos += far_cos * here[:, 0:LANES] - far_sin * here[:, LANES:]
                coeff_sin += far_sin * here[:, 0:LANES] + far_cos * here[:, LANES:]
            ratio = wave_f / TRUNC
            weight = jnp.where((wave == 0) | (2 * wave == length_int), 1.0, 2.0)
            weight = jnp.where(2 * wave <= length_int, weight, 0.0)
            damping = weight / ((1.0 + diffusion * (ratio * ratio)) * length)
            amp_cos = coeff_cos * damping
            amp_sin = coeff_sin * damping
            for far in range(FAR):
                far_cos, far_sin = base(24 + far)
                part = jnp.concatenate(
                    [
                        amp_cos * far_cos + amp_sin * far_sin,
                        amp_sin * far_cos - amp_cos * far_sin,
                    ],
                    axis=1,
                )
                p_ref[CH * far : CH * (far + 1), pl.ds(column, 2 * LANES)] = part.astype(BF16)
            return carry

        lax.fori_loop(0, K_BLOCKS, block_step, 0)
        half = slice(turn * 2 * TRUNC, (turn + 1) * 2 * TRUNC)
        y_ref[turn] = lax.dot_general(
            p_ref[:, half], w_ref[:, half], (((1,), (1,)), ((), ())), preferred_element_type=F32
        )

    lane = lane_iota(8)
    bounds = [lane * N_LON - length_int for length_int in lengths]

    def out_step(far, carry):
        at = pl.multiple_of(far * CH, CH)
        for near in range(NEAR):
            l = far * NEAR + near
            lanes = slice(LANES * near, LANES * (near + 1))
            pieces = []
            for turn in range(2):
                inside = bounds[turn] + l < 0
                here = y_ref[turn, pl.ds(at, CH), lanes]
                pieces.append([jnp.where(inside, here[0:8], 0.0), jnp.where(inside, here[8:16], 0.0)])
            main = [jnp.where(left, pieces[0][h], pltpu.roll(pieces[1][h], 64, 1)) for h in range(2)]
            out_ref[l, 0:CH, :] = jnp.concatenate(main, axis=0).astype(BF16)
            tail = jnp.where(
                lane < TAIL,
                pltpu.roll(pieces[0][0], 64, 1),
                jnp.where(
                    lane < 64,
                    pltpu.roll(pieces[1][0], 64 + TAIL, 1),
                    jnp.where(lane < 64 + TAIL, pieces[0][1], pltpu.roll(pieces[1][1], TAIL, 1)),
                ),
            )
            out_ref[l, CH : CH + 8, :] = tail.astype(BF16)
        return carry

    lax.fori_loop(0, FAR, out_step, 0, unroll=2)


def final_kernel(in_ref, out_ref):
    lane = lane_iota(CH).astype(F32).astype(BF16)
    tiles = {}

    def place(source, source_lane, begin, width):
        tile, lane_at = begin // LANES, begin % LANES
        moved = pltpu.roll(source, (lane_at - source_lane) % LANES, 1)
        if tile in tiles:
            tiles[tile] = jnp.where(lane >= lane_at, moved, tiles[tile])
        else:
            tiles[tile] = moved
        if lane_at + width >= LANES:
            out_ref[:, tile * LANES : (tile + 1) * LANES] = tiles.pop(tile)
            if lane_at + width > LANES:
                tiles[tile + 1] = moved

    for d in range(N_LON):
        main = in_ref[d, 0:CH, :]
        tail = in_ref[d, CH : CH + 8, :].astype(F32)
        tail = jnp.concatenate([tail, pltpu.roll(tail, 64, 1)], axis=0).astype(BF16)
        for turn in range(2):
            begin = SLOTS * (2 * d + turn)
            place(main, HEAD * turn, begin, HEAD)
            place(tail, TAIL * turn, begin + HEAD, TAIL)


def vmem():
    return pl.BlockSpec(memory_space=pltpu.VMEM)


def smem():
    return pl.BlockSpec(memory_space=pltpu.SMEM)


def shape(dims, dtype=BF16):
    return pltpu.VMEM(dims, dtype)


def near(x):
    return pltpu.with_memory_space_constraint(x, pltpu.VMEM)


def exchange(blocks):
    return lax.all_to_all(blocks, "lon", split_axis=0, concat_axis=0, tiled=True)


def on_device(field, dep_frac, dep_index, send_list, send_count, cycle_len, diffusion):
    lon_index = lax.axis_index("lon")
    bands = lax.axis_size("lat")
    toward_before, toward_after = pl.pallas_call(
        pick_kernel,
        out_shape=(shape((CH, HALO)), shape((CH, HALO))),
        in_specs=[smem(), smem(), smem(), vmem()],
        out_specs=(vmem(), vmem()),
        name="pick_blocks",
    )(send_list, send_count, cycle_len, field)
    north = lax.ppermute(toward_after, "lat", [(i, i + 1) for i in range(bands - 1)])
    south = lax.ppermute(toward_before, "lat", [(i + 1, i) for i in range(bands - 1)])

    windows, stencil = pl.pallas_call(
        prepare_kernel,
        out_shape=(shape((CH * OWN_WIN, WINDOW)), shape((2, OWN), F32)),
        in_specs=[smem(), vmem(), vmem(), vmem()],
        out_specs=(vmem(), vmem()),
        scratch_shapes=[
            pltpu.VMEM((CH, OWN + LANES), BF16),
            pltpu.VMEM((8, OWN + LANES), F32),
        ],
        name="prepare",
    )(cycle_len, field, dep_index, dep_frac.reshape(1, OWN))

    departed = pl.pallas_call(
        gather_kernel,
        out_shape=shape((N_LON, CH + 8, LANES)),
        in_specs=[vmem(), vmem(), vmem(), vmem()],
        out_specs=vmem(),
        scratch_shapes=[
            pltpu.VMEM((CH, RIM), BF16),
            pltpu.VMEM((CH * N_WIN, WINDOW), BF16),
            pltpu.VMEM((WINDOW, BATCH), BF16),
            pltpu.VMEM((WINDOW, BATCH), BF16),
            pltpu.VMEM((CH, OWN - MAIN_COLS), F32),
        ],
        name="departure_gather",
    )(near(windows), near(north), near(south), near(stencil))

    received = exchange(departed)

    filtered = pl.pallas_call(
        spectral_kernel,
        out_shape=shape((N_LON, CH + 8, LANES)),
        in_specs=[smem(), smem(), vmem()],
        out_specs=vmem(),
        scratch_shapes=[
            pltpu.VMEM((FAR * CH, NEAR * LANES), BF16),
            pltpu.VMEM((FAR * CH, NEAR * LANES), BF16),
            pltpu.VMEM((NEAR * LANES, 4 * TRUNC), BF16),
            pltpu.VMEM((48, 2 * LANES), F32),
            pltpu.VMEM((FAR * CH, 4 * TRUNC), BF16),
            pltpu.VMEM((2, FAR * CH, NEAR * LANES), F32),
        ],
        name="zonal_filter",
    )(cycle_len, diffusion, near(received))

    landed = exchange(filtered)

    return pl.pallas_call(
        final_kernel,
        out_shape=jax.ShapeDtypeStruct((CH, OWN), BF16),
        in_specs=[vmem()],
        out_specs=vmem(),
        name="unpack_columns",
    )(near(landed))


def solution(mesh):
    placed = (
        P(None, ("lat", "lon")),
        P(("lat", "lon")),
        P(None, ("lat", "lon")),
        P(("lat", "lon"), None, None),
        P(("lat", "lon"), None),
        P("lat", None),
        P(),
    )
    return jax.shard_map(
        on_device, mesh=mesh, in_specs=placed, out_specs=P(None, ("lat", "lon")), check_vma=False
    )
```

```python
import math

import jax
import jax.numpy as jnp
from jax import lax
from jax.experimental import pallas as pl
from jax.experimental.pallas import tpu as pltpu
from jax.sharding import PartitionSpec as P

TRUNC = 640
HALO_BLOCKS = 8
CH = 16
CYCLES = 128
SLOTS = 81
N_LON = 64
OWN = CYCLES * SLOTS
HALO = HALO_BLOCKS * SLOTS
LANES = 128
STRIDE = 255
WINDOW = 256
EXT = OWN + 2 * HALO
N_WIN = (EXT - 2) // STRIDE + 1
HEAD = 64
TAIL = SLOTS - HEAD
SLOT_ROWS = 96
MAIN_COLS = N_LON * LANES
K_BLOCKS = TRUNC // LANES
OWN_WIN = OWN // STRIDE + 1
RIM_OWN = OWN - STRIDE * (OWN_WIN - 1)
RIM = -(-(STRIDE * (N_WIN - OWN_WIN) + WINDOW) // LANES) * LANES
BATCH = 2 * WINDOW
MAIN_STEPS = MAIN_COLS // BATCH
FULL_STEPS = OWN // BATCH
OUT_PARTS = 9
NEAR = 4
FAR = N_LON // NEAR
F32 = jnp.float32
BF16 = jnp.bfloat16


def lane_iota(rows, cols=LANES):
    return lax.broadcasted_iota(jnp.int32, (rows, cols), 1)


def slots_used(length, lon_index):
    return (length - lon_index + (N_LON - 1)) >> 6


def pick_kernel(list_ref, count_ref, len_ref, field_ref, first_ref, second_ref):
    lon_index = lax.axis_index("lon")
    lane = lane_iota(CH, 2 * LANES)
    parity = lax.axis_index("lat") & 1
    for way, out_ref in ((parity, first_ref), (1 - parity, second_ref)):
        blocks = [jnp.zeros((CH, LANES), F32) for _ in range(7)]
        for k in range(HALO_BLOCKS):
            row = jnp.clip(list_ref[0, way, k], 0, CYCLES - 1)
            start = row * SLOTS
            base = jnp.minimum(start >> 7, OWN // LANES - 2)
            shift = start - base * LANES
            place = (SLOTS * k) % LANES
            block = (SLOTS * k) // LANES
            window = field_ref[:, pl.ds(pl.multiple_of(base * LANES, LANES), 2 * LANES)]
            moved = pltpu.roll(window.astype(F32), (place - shift + 2 * LANES) & 255, 1)
            used = jnp.where(k < count_ref[0, way], slots_used(len_ref[0, row], lon_index), 0)
            keep = (lane >= place) & (lane < place + used)
            for half in range(2):
                part = slice(half * LANES, (half + 1) * LANES)
                blocks[block + half] = jnp.where(keep[:, part], moved[:, part], blocks[block + half])
        for i in range(5):
            out_ref[:, i * LANES : (i + 1) * LANES] = blocks[i].astype(BF16)
        out_ref[:, 5 * LANES : HALO] = blocks[5][:, : HALO - 5 * LANES].astype(BF16)


def prepare_kernel(
    len_ref, diff_ref, field_ref, index_ref, frac_ref, win_ref, where_ref, numbers_ref, ext_ref, pair_ref
):
    lon_index = lax.axis_index("lon")
    for turn in range(2):
        length = jnp.full((1, LANES), len_ref[0, 2 * lon_index + turn], jnp.int32)
        numbers_ref[CH + turn : CH + turn + 1, :] = length.astype(F32)
    for c in range(CH):
        numbers_ref[c : c + 1, :] = jnp.full((1, LANES), diff_ref[c], F32)
    pair_ref[:, OWN:] = jnp.zeros((8, LANES), F32)
    pair_ref[0:1, 0:OWN] = index_ref[0:1, :].astype(F32)
    for b in range(OWN // LANES):
        pair_ref[1:2, b * LANES : (b + 1) * LANES] = frac_ref[b : b + 1, :]
    lane = lane_iota(8)
    tile = None
    for d in range(N_LON):
        used = [slots_used(len_ref[0, 2 * d + turn], lon_index) for turn in range(2)]
        begin = 2 * SLOTS * d
        here = jnp.where(
            lane < HEAD,
            pair_ref[:, begin : begin + LANES],
            pair_ref[:, begin + TAIL : begin + TAIL + LANES],
        )
        limit = jnp.where(lane < HEAD, used[0], used[1] + HEAD)
        here = jnp.where(lane < limit, here, -1.0)
        where_ref[:, LANES * d : LANES * (d + 1)] = here[0:2]
        for turn in range(2):
            at = TAIL * (2 * d + turn)
            number, place = at // LANES, at % LANES
            source = begin + SLOTS * turn + HEAD - place
            limit = place + used[turn] - HEAD
            here = jnp.where(lane < limit, pair_ref[:, source : source + LANES], -1.0)
            tile = here if tile is None else jnp.where(lane >= place, here, tile)
            if place + TAIL >= LANES:
                column = MAIN_COLS + LANES * number
                where_ref[:, column : column + LANES] = tile[0:2]
                tile = None
                if place + TAIL > LANES:
                    source += LANES
                    tile = jnp.where(lane < limit - LANES, pair_ref[:, source : source + LANES], -1.0)

    lane = lane_iota(CH)
    for b in range(OWN // LANES):
        first = (LANES * b) // SLOTS
        last = (LANES * b + LANES - 1) // SLOTS
        limit = SLOTS * last + slots_used(len_ref[0, last], lon_index) - LANES * b
        limit = jnp.full((CH, LANES), limit, jnp.int32)
        for r in range(last - 1, first - 1, -1):
            here = SLOTS * r + slots_used(len_ref[0, r], lon_index) - LANES * b
            limit = jnp.where(lane < SLOTS * (r + 1) - LANES * b, here, limit)
        keep = jnp.where(lane < limit, 1.0, 0.0).astype(BF16)
        part = slice(b * LANES, (b + 1) * LANES)
        ext_ref[:, part] = field_ref[:, part] * keep
    ext_ref[:, OWN : OWN + LANES] = jnp.zeros((CH, LANES), BF16)
    for q in range(OWN_WIN):
        win_ref[CH * q : CH * (q + 1), :] = ext_ref[:, STRIDE * q : STRIDE * q + WINDOW]


def gather_kernel(own_ref, outer_ref, inner_ref, where_ref, out_ref, rim_ref, win_ref, m0, m1, tail_ref):
    rim_ref[:, RIM_OWN + 2 * HALO :] = jnp.zeros((CH, RIM - RIM_OWN - 2 * HALO), BF16)
    rim_ref[:, 0:RIM_OWN] = own_ref[CH * (OWN_WIN - 1) : CH * OWN_WIN, 0:RIM_OWN]
    even = (lax.axis_index("lat") & 1) == 0

    @pl.when(even)
    def _():
        rim_ref[:, RIM_OWN : RIM_OWN + HALO] = outer_ref[...]
        rim_ref[:, RIM_OWN + HALO : RIM_OWN + 2 * HALO] = inner_ref[...]

    @pl.when(jnp.logical_not(even))
    def _():
        rim_ref[:, RIM_OWN : RIM_OWN + HALO] = inner_ref[...]
        rim_ref[:, RIM_OWN + HALO : RIM_OWN + 2 * HALO] = outer_ref[...]

    win_ref[0 : CH * (OWN_WIN - 1), :] = own_ref[0 : CH * (OWN_WIN - 1), :]
    for q in range(OWN_WIN - 1, N_WIN):
        at = STRIDE * (q - OWN_WIN + 1)
        win_ref[CH * q : CH * (q + 1), :] = rim_ref[:, at : at + WINDOW]

    def window_number(start, width):
        index = where_ref[0:1, pl.ds(start, width)].astype(jnp.int32)
        return index, (index * 32897) >> 23

    def make_weights(start, width, m_ref):
        index, number = window_number(start, width)
        frac = where_ref[1:2, pl.ds(start, width)]
        used = index >= 0
        offset = (index - STRIDE * number).astype(F32)
        offset = jnp.broadcast_to(offset, (16, width)).astype(BF16)
        low = jnp.broadcast_to(jnp.where(used, 1.0 - frac, 0.0), (16, width)).astype(BF16)
        high = jnp.broadcast_to(jnp.where(used, frac, 0.0), (16, width)).astype(BF16)
        row16 = lax.broadcasted_iota(jnp.int32, (16, width), 0).astype(F32)
        for s in range(WINDOW // 16):
            row = (row16 + 16.0 * s).astype(BF16)
            before = (row16 + (16.0 * s - 1.0)).astype(BF16)
            m_ref[16 * s : 16 * (s + 1), 0:width] = jnp.where(
                row == offset, low, jnp.where(before == offset, high, jnp.zeros_like(low))
            )

    def choose(start, width, m_ref):
        windows = jnp.dot(win_ref[...], m_ref[:, 0:width], preferred_element_type=F32)
        index, number = window_number(start, width)
        number = jnp.broadcast_to(number, (CH, width))
        bits = [(number & (1 << i)) != 0 for i in range(6)]

        def pick(low, level):
            if level == 0:
                return windows[CH * low : CH * (low + 1)]
            near = pick(low, level - 1)
            far = low + (1 << (level - 1))
            if far >= N_WIN:
                return near
            return jnp.where(bits[level - 1], pick(far, level - 1), near)

        return pick(0, 6)

    buffers = (m0, m1)
    make_weights(0, BATCH, m0)
    for step in range(FULL_STEPS):
        if step + 1 < FULL_STEPS:
            make_weights((step + 1) * BATCH, BATCH, buffers[(step + 1) % 2])
        total = choose(step * BATCH, BATCH, buffers[step % 2])
        if step < MAIN_STEPS:
            total = total.astype(BF16)
            for i in range(BATCH // LANES):
                lanes = slice(i * LANES, (i + 1) * LANES)
                out_ref[BATCH // LANES * step + i, 0:CH, :] = total[:, lanes]
        else:
            at = step * BATCH - MAIN_COLS
            tail_ref[:, at : at + BATCH] = total
    rest = FULL_STEPS * BATCH
    make_weights(rest, OWN - rest, m0)
    tail_ref[:, rest - MAIN_COLS :] = choose(rest, OWN - rest, m0)

    left = lane_iota(8) < 64
    for d in range(N_LON):
        at = 2 * TAIL * d
        tile, place = at // LANES, at % LANES
        halves = []
        for h in range(2):
            rows = slice(8 * h, 8 * h + 8)
            here = tail_ref[rows, tile * LANES : (tile + 1) * LANES]
            if place + 2 * TAIL > LANES:
                there = tail_ref[rows, (tile + 1) * LANES : (tile + 2) * LANES]
                here = jnp.where(lane_iota(8) >= place, here, there)
            halves.append(pltpu.roll(here, (64 * h - place) % LANES, 1))
        out_ref[d, CH : CH + 8, :] = jnp.where(left, halves[0], halves[1]).astype(BF16)


def cos_sin(product, length, inverse):
    turns = product - jnp.round(product * inverse) * length
    half = turns * (inverse * math.pi)
    z = half * half
    s = -1.0 / 39916800.0
    for c in (1.0 / 362880.0, -1.0 / 5040.0, 1.0 / 120.0, -1.0 / 6.0, 1.0):
        s = s * z + c
    s = s * half
    c0 = 1.0 / 479001600.0
    for c in (-1.0 / 3628800.0, 1.0 / 40320.0, -1.0 / 720.0, 1.0 / 24.0, -0.5, 1.0):
        c0 = c0 * z + c
    return 1.0 - 2.0 * s * s, 2.0 * s * c0


def rotate(cosine, sine, by_cos, by_sin):
    return cosine * by_cos - sine * by_sin, sine * by_cos + cosine * by_sin


def spectral_kernel(numbers_ref, in_ref, out_ref, x0, x1, w_ref, base_ref, p_ref, y_ref):
    lengths = [numbers_ref[CH + turn : CH + turn + 1, :] for turn in range(2)]
    diffusion = numbers_ref[0:CH, :]
    for near in range(NEAR):
        w_ref[LANES * near + SLOT_ROWS : LANES * (near + 1), :] = jnp.zeros(
            (LANES - SLOT_ROWS, 4 * TRUNC), BF16
        )
    left = lane_iota(8) < 64

    for far in range(FAR):
        rows = slice(CH * far, CH * (far + 1))
        for near in range(NEAR):
            l = far * NEAR + near
            main = in_ref[l, 0:CH, :].astype(F32)
            tail = in_ref[l, CH : CH + 8, :].astype(F32)
            swap = pltpu.roll(main, 64, 1)
            first = [
                jnp.where(left, main[0:8], pltpu.roll(tail, 64, 1)),
                jnp.where(left, main[8:16], tail),
            ]
            second = [
                jnp.where(left, swap[0:8], pltpu.roll(tail, HEAD - TAIL, 1)),
                jnp.where(left, swap[8:16], pltpu.roll(tail, LANES - TAIL, 1)),
            ]
            lanes = slice(LANES * near, LANES * (near + 1))
            x0[rows, lanes] = jnp.concatenate(first, axis=0).astype(BF16)
            x1[rows, lanes] = jnp.concatenate(second, axis=0).astype(BF16)

    first_row = lax.broadcasted_iota(jnp.int32, (8, LANES), 0) == 0
    i48 = lax.broadcasted_iota(jnp.int32, (48, LANES), 0)
    factor = jnp.where(
        i48 < 8,
        N_LON * i48,
        jnp.where(i48 < 24, 8 * N_LON * (i48 - 8), jnp.where(i48 < 40, NEAR * (i48 - 24), i48 - 40)),
    ).astype(F32)

    for turn in range(2):
        length = lengths[turn]
        inverse = 1.0 / length
        x_ref = (x0, x1)[turn]
        for block in range(K_BLOCKS):
            wave_f = (lane_iota(1) + block * LANES).astype(F32)
            base_at = base_ref.at[(turn * K_BLOCKS + block) % 2]
            columns = slice(
                (turn * K_BLOCKS + block) * 2 * LANES, (turn * K_BLOCKS + block + 1) * 2 * LANES
            )
            cosine, sine = cos_sin(factor * wave_f, length, inverse)
            base_at[:, 0:LANES] = cosine
            base_at[:, LANES : 2 * LANES] = sine

            def base(i, base_at=base_at):
                return base_at[i : i + 1, 0:LANES], base_at[i : i + 1, LANES : 2 * LANES]

            low_cos, low_sin = cosine[0:8], sine[0:8]
            for pair in range(SLOT_ROWS // 16):
                strips = [rotate(low_cos, low_sin, *base(8 + 2 * pair + h)) for h in range(2)]
                if pair == SLOT_ROWS // 16 - 1:
                    strips[0] = [jnp.where(first_row, v, 0.0) for v in strips[0]]
                    strips[1] = [jnp.zeros_like(v) for v in strips[1]]
                for near in range(NEAR):
                    turned = strips if near == 0 else [rotate(*st, *base(40 + near)) for st in strips]
                    both = jnp.concatenate(
                        [
                            jnp.concatenate([turned[0][0], turned[1][0]], axis=0),
                            jnp.concatenate([turned[0][1], turned[1][1]], axis=0),
                        ],
                        axis=1,
                    )
                    at = LANES * near + 16 * pair
                    w_ref[at : at + 16, columns] = both.astype(BF16)
            partial = jnp.dot(x_ref[...], w_ref[:, columns], preferred_element_type=F32)
            coeff_cos = jnp.zeros((CH, LANES), F32)
            coeff_sin = jnp.zeros((CH, LANES), F32)
            for far in range(FAR):
                here = partial[CH * far : CH * (far + 1)]
                far_cos, far_sin = base(24 + far)
                coeff_cos += far_cos * here[:, 0:LANES] - far_sin * here[:, LANES:]
                coeff_sin += far_sin * here[:, 0:LANES] + far_cos * here[:, LANES:]
            ratio = wave_f / TRUNC
            weight = jnp.where((wave_f == 0.0) | (2.0 * wave_f == length), 1.0, 2.0)
            weight = jnp.where(2.0 * wave_f <= length, weight, 0.0)
            damping = weight / ((1.0 + diffusion * (ratio * ratio)) * length)
            amp_cos = coeff_cos * damping
            amp_sin = coeff_sin * damping
            for far in range(FAR):
                far_cos, far_sin = base(24 + far)
                part = jnp.concatenate(
                    [
                        amp_cos * far_cos + amp_sin * far_sin,
                        amp_sin * far_cos - amp_cos * far_sin,
                    ],
                    axis=1,
                )
                p_ref[CH * far : CH * (far + 1), columns] = part.astype(BF16)
        half = slice(turn * 2 * TRUNC, (turn + 1) * 2 * TRUNC)
        y_ref[turn] = lax.dot_general(
            p_ref[:, half], w_ref[:, half], (((1,), (1,)), ((), ())), preferred_element_type=F32
        )

    lane = lane_iota(8)
    bounds = [(lane * N_LON).astype(F32) - length for length in lengths]

    for far in range(FAR):
        rows = slice(CH * far, CH * (far + 1))
        for near in range(NEAR):
            l = far * NEAR + near
            lanes = slice(LANES * near, LANES * (near + 1))
            pieces = []
            for turn in range(2):
                inside = bounds[turn] < float(-l)
                here = y_ref[turn, rows, lanes]
                pieces.append([jnp.where(inside, here[0:8], 0.0), jnp.where(inside, here[8:16], 0.0)])
            main = [jnp.where(left, pieces[0][h], pltpu.roll(pieces[1][h], 64, 1)) for h in range(2)]
            out_ref[l, 0:CH, :] = jnp.concatenate(main, axis=0).astype(BF16)
            tail = jnp.where(
                lane < TAIL,
                pltpu.roll(pieces[0][0], 64, 1),
                jnp.where(
                    lane < 64,
                    pltpu.roll(pieces[1][0], 64 + TAIL, 1),
                    jnp.where(lane < 64 + TAIL, pieces[0][1], pltpu.roll(pieces[1][1], TAIL, 1)),
                ),
            )
            out_ref[l, CH : CH + 8, :] = tail.astype(BF16)


def final_kernel(in_ref, out_hbm, out_ref, sems):
    part_tiles = OWN // LANES // OUT_PARTS

    def part_copy(part):
        columns = slice(part * part_tiles * LANES, (part + 1) * part_tiles * LANES)
        return pltpu.make_async_copy(out_ref.at[:, columns], out_hbm.at[:, columns], sems.at[part])

    lane = lane_iota(CH).astype(F32).astype(BF16)
    tiles = {}

    def place(source, source_lane, begin, width):
        tile, lane_at = begin // LANES, begin % LANES
        moved = pltpu.roll(source, (lane_at - source_lane) % LANES, 1)
        if tile in tiles:
            tiles[tile] = jnp.where(lane >= lane_at, moved, tiles[tile])
        else:
            tiles[tile] = moved
        if lane_at + width >= LANES:
            out_ref[:, tile * LANES : (tile + 1) * LANES] = tiles.pop(tile)
            if (tile + 1) % part_tiles == 0:
                part_copy(tile // part_tiles).start()
            if lane_at + width > LANES:
                tiles[tile + 1] = moved

    for d in range(N_LON):
        main = in_ref[d, 0:CH, :]
        tail = in_ref[d, CH : CH + 8, :].astype(F32)
        tail = jnp.concatenate([tail, pltpu.roll(tail, 64, 1)], axis=0).astype(BF16)
        for turn in range(2):
            begin = SLOTS * (2 * d + turn)
            place(main, HEAD * turn, begin, HEAD)
            place(tail, TAIL * turn, begin + HEAD, TAIL)
    for part in range(OUT_PARTS):
        part_copy(part).wait()


def vmem():
    return pl.BlockSpec(memory_space=pltpu.VMEM)


def smem():
    return pl.BlockSpec(memory_space=pltpu.SMEM)


def shape(dims, dtype=BF16):
    return pltpu.VMEM(dims, dtype)


def near(x):
    return pltpu.with_memory_space_constraint(x, pltpu.VMEM)


def exchange(blocks):
    return lax.all_to_all(blocks, "lon", split_axis=0, concat_axis=0, tiled=True)


def on_device(field, dep_frac, dep_index, send_list, send_count, cycle_len, diffusion):
    lon_index = lax.axis_index("lon")
    bands = lax.axis_size("lat")
    outward, inward = pl.pallas_call(
        pick_kernel,
        out_shape=(shape((CH, HALO)), shape((CH, HALO))),
        in_specs=[smem(), smem(), smem(), vmem()],
        out_specs=(vmem(), vmem()),
        name="pick_blocks",
    )(send_list, send_count, cycle_len, field)
    pairs = [(i, i + 1) for i in range(1, bands - 1, 2)]
    from_outer = lax.ppermute(outward, "lat", pairs + [(j, i) for i, j in pairs])
    pairs = [(i, i + 1) for i in range(0, bands - 1, 2)]
    from_inner = lax.ppermute(inward, "lat", pairs + [(j, i) for i, j in pairs])

    windows, stencil, numbers = pl.pallas_call(
        prepare_kernel,
        out_shape=(shape((CH * OWN_WIN, WINDOW)), shape((2, OWN), F32), shape((CH + 8, LANES), F32)),
        in_specs=[smem(), smem(), vmem(), vmem(), vmem()],
        out_specs=(vmem(), vmem(), vmem()),
        scratch_shapes=[
            pltpu.VMEM((CH, OWN + LANES), BF16),
            pltpu.VMEM((8, OWN + LANES), F32),
        ],
        name="prepare",
    )(cycle_len, diffusion, near(field), dep_index, dep_frac.reshape(OWN // LANES, LANES))

    departed = pl.pallas_call(
        gather_kernel,
        out_shape=shape((N_LON, CH + 8, LANES)),
        in_specs=[vmem(), vmem(), vmem(), vmem()],
        out_specs=vmem(),
        scratch_shapes=[
            pltpu.VMEM((CH, RIM), BF16),
            pltpu.VMEM((CH * N_WIN, WINDOW), BF16),
            pltpu.VMEM((WINDOW, BATCH), BF16),
            pltpu.VMEM((WINDOW, BATCH), BF16),
            pltpu.VMEM((CH, OWN - MAIN_COLS), F32),
        ],
        name="departure_gather",
    )(near(windows), near(from_outer), near(from_inner), near(stencil))

    received = exchange(departed)

    filtered = pl.pallas_call(
        spectral_kernel,
        out_shape=shape((N_LON, CH + 8, LANES)),
        in_specs=[vmem(), vmem()],
        out_specs=vmem(),
        scratch_shapes=[
            pltpu.VMEM((FAR * CH, NEAR * LANES), BF16),
            pltpu.VMEM((FAR * CH, NEAR * LANES), BF16),
            pltpu.VMEM((NEAR * LANES, 4 * TRUNC), BF16),
            pltpu.VMEM((2, 48, 2 * LANES), F32),
            pltpu.VMEM((FAR * CH, 4 * TRUNC), BF16),
            pltpu.VMEM((2, FAR * CH, NEAR * LANES), F32),
        ],
        name="zonal_filter",
    )(near(numbers), near(received))

    landed = exchange(filtered)

    return pl.pallas_call(
        final_kernel,
        out_shape=jax.ShapeDtypeStruct((CH, OWN), BF16),
        in_specs=[vmem()],
        out_specs=pl.BlockSpec(memory_space=pl.ANY),
        scratch_shapes=[pltpu.VMEM((CH, OWN), BF16), pltpu.SemaphoreType.DMA((OUT_PARTS,))],
        name="unpack_columns",
    )(near(landed))


def solution(mesh):
    placed = (
        P(None, ("lat", "lon")),
        P(("lat", "lon")),
        P(None, ("lat", "lon")),
        P(("lat", "lon"), None, None),
        P(("lat", "lon"), None),
        P("lat", None),
        P(),
    )
    return jax.shard_map(
        on_device, mesh=mesh, in_specs=placed, out_specs=P(None, ("lat", "lon")), check_vma=False
    )
```

```python
import math

import jax
import jax.numpy as jnp
from jax import lax
from jax.experimental import pallas as pl
from jax.experimental.pallas import tpu as pltpu
from jax.sharding import PartitionSpec as P

TRUNC = 640
HALO_BLOCKS = 8
CH = 16
CYCLES = 128
SLOTS = 81
N_LON = 64
OWN = CYCLES * SLOTS
HALO = HALO_BLOCKS * SLOTS
LANES = 128
STRIDE = 255
WINDOW = 256
EXT = OWN + 2 * HALO
N_WIN = (EXT - 2) // STRIDE + 1
HEAD = 64
TAIL = SLOTS - HEAD
SLOT_ROWS = 96
MAIN_COLS = N_LON * LANES
K_BLOCKS = TRUNC // LANES
OWN_WIN = OWN // STRIDE + 1
RIM_OWN = OWN - STRIDE * (OWN_WIN - 1)
RIM = -(-(STRIDE * (N_WIN - OWN_WIN) + WINDOW) // LANES) * LANES
BATCH = 2 * WINDOW
MAIN_STEPS = MAIN_COLS // BATCH
FULL_STEPS = OWN // BATCH
OUT_PARTS = 9
NEAR = 4
FAR = N_LON // NEAR
F32 = jnp.float32
BF16 = jnp.bfloat16


def lane_iota(rows, cols=LANES):
    return lax.broadcasted_iota(jnp.int32, (rows, cols), 1)


def slots_used(length, lon_index):
    return (length - lon_index + (N_LON - 1)) >> 6


def pick_kernel(
    list_ref, count_ref, len_ref, diff_ref, len_row, field_ref, index_ref, frac_ref,
    first_ref, second_ref, field_out, index_out, frac_out, len_out, numbers_ref,
):
    len_out[...] = len_row[...]
    field_out[...] = field_ref[...]
    index_out[...] = index_ref[...]
    frac_out[...] = frac_ref[...]
    lon_index = lax.axis_index("lon")
    lane = lane_iota(CH, 2 * LANES)
    for turn in range(2):
        length = jnp.full((1, LANES), len_ref[0, 2 * lon_index + turn], jnp.int32)
        numbers_ref[CH + turn : CH + turn + 1, :] = length.astype(F32)
    for c in range(CH):
        numbers_ref[c : c + 1, :] = jnp.full((1, LANES), diff_ref[c], F32)
    parity = lax.axis_index("lat") & 1
    for way, out_ref in ((parity, first_ref), (1 - parity, second_ref)):
        blocks = [jnp.zeros((CH, LANES), F32) for _ in range(7)]
        for k in range(HALO_BLOCKS):
            row = jnp.clip(list_ref[0, way, k], 0, CYCLES - 1)
            start = row * SLOTS
            base = jnp.minimum(start >> 7, OWN // LANES - 2)
            shift = start - base * LANES
            place = (SLOTS * k) % LANES
            block = (SLOTS * k) // LANES
            window = field_ref[:, pl.ds(pl.multiple_of(base * LANES, LANES), 2 * LANES)]
            moved = pltpu.roll(window.astype(F32), (place - shift + 2 * LANES) & 255, 1)
            used = jnp.where(k < count_ref[0, way], slots_used(len_ref[0, row], lon_index), 0)
            keep = (lane >= place) & (lane < place + used)
            for half in range(2):
                part = slice(half * LANES, (half + 1) * LANES)
                blocks[block + half] = jnp.where(keep[:, part], moved[:, part], blocks[block + half])
        for i in range(5):
            out_ref[:, i * LANES : (i + 1) * LANES] = blocks[i].astype(BF16)
        out_ref[:, 5 * LANES : HALO] = blocks[5][:, : HALO - 5 * LANES].astype(BF16)


def prepare_kernel(len_ref, field_ref, index_ref, frac_ref, win_ref, where_ref, ext_ref, pair_ref):
    all_used = slots_used(len_ref[...], lax.axis_index("lon"))
    used_slots = [jnp.broadcast_to(all_used[:, r : r + 1], (8, LANES)) for r in range(CYCLES)]
    pair_ref[:, OWN:] = jnp.zeros((8, LANES), F32)
    pair_ref[0:1, 0:OWN] = index_ref[0:1, :].astype(F32)
    for b in range(OWN // LANES):
        pair_ref[1:2, b * LANES : (b + 1) * LANES] = frac_ref[b : b + 1, :]
    lane = lane_iota(8)
    tile = None
    for d in range(N_LON):
        used = used_slots[2 * d : 2 * d + 2]
        begin = 2 * SLOTS * d
        here = jnp.where(
            lane < HEAD,
            pair_ref[:, begin : begin + LANES],
            pair_ref[:, begin + TAIL : begin + TAIL + LANES],
        )
        limit = jnp.where(lane < HEAD, used[0], used[1] + HEAD)
        here = jnp.where(lane < limit, here, -1.0)
        where_ref[:, LANES * d : LANES * (d + 1)] = here[0:2]
        for turn in range(2):
            at = TAIL * (2 * d + turn)
            number, place = at // LANES, at % LANES
            source = begin + SLOTS * turn + HEAD - place
            limit = place + used[turn] - HEAD
            here = jnp.where(lane < limit, pair_ref[:, source : source + LANES], -1.0)
            tile = here if tile is None else jnp.where(lane >= place, here, tile)
            if place + TAIL >= LANES:
                column = MAIN_COLS + LANES * number
                where_ref[:, column : column + LANES] = tile[0:2]
                tile = None
                if place + TAIL > LANES:
                    source += LANES
                    tile = jnp.where(lane < limit - LANES, pair_ref[:, source : source + LANES], -1.0)

    for b in range(OWN // LANES):
        first = (LANES * b) // SLOTS
        last = (LANES * b + LANES - 1) // SLOTS
        limit = used_slots[last] + (SLOTS * last - LANES * b)
        for r in range(last - 1, first - 1, -1):
            here = used_slots[r] + (SLOTS * r - LANES * b)
            limit = jnp.where(lane < SLOTS * (r + 1) - LANES * b, here, limit)
        keep = jnp.where(lane < limit, 1.0, 0.0)
        keep = jnp.concatenate([keep, keep], axis=0).astype(BF16)
        part = slice(b * LANES, (b + 1) * LANES)
        ext_ref[:, part] = field_ref[:, part] * keep
    ext_ref[:, OWN : OWN + LANES] = jnp.zeros((CH, LANES), BF16)
    for q in range(OWN_WIN):
        win_ref[CH * q : CH * (q + 1), :] = ext_ref[:, STRIDE * q : STRIDE * q + WINDOW]


def gather_kernel(own_ref, outer_ref, inner_ref, where_ref, out_ref, rim_ref, win_ref, m0, m1, tail_ref):
    rim_ref[:, RIM_OWN + 2 * HALO :] = jnp.zeros((CH, RIM - RIM_OWN - 2 * HALO), BF16)
    rim_ref[:, 0:RIM_OWN] = own_ref[CH * (OWN_WIN - 1) : CH * OWN_WIN, 0:RIM_OWN]
    even = (lax.axis_index("lat") & 1) == 0

    @pl.when(even)
    def _():
        rim_ref[:, RIM_OWN : RIM_OWN + HALO] = outer_ref[...]
        rim_ref[:, RIM_OWN + HALO : RIM_OWN + 2 * HALO] = inner_ref[...]

    @pl.when(jnp.logical_not(even))
    def _():
        rim_ref[:, RIM_OWN : RIM_OWN + HALO] = inner_ref[...]
        rim_ref[:, RIM_OWN + HALO : RIM_OWN + 2 * HALO] = outer_ref[...]

    win_ref[0 : CH * (OWN_WIN - 1), :] = own_ref[0 : CH * (OWN_WIN - 1), :]
    for q in range(OWN_WIN - 1, N_WIN):
        at = STRIDE * (q - OWN_WIN + 1)
        win_ref[CH * q : CH * (q + 1), :] = rim_ref[:, at : at + WINDOW]

    def window_number(start, width):
        index = where_ref[0:1, pl.ds(start, width)].astype(jnp.int32)
        return index, (index * 32897) >> 23

    def make_weights(start, width, m_ref):
        index, number = window_number(start, width)
        frac = where_ref[1:2, pl.ds(start, width)]
        used = index >= 0
        offset = (index - STRIDE * number).astype(F32)
        offset = jnp.broadcast_to(offset, (16, width)).astype(BF16)
        low = jnp.broadcast_to(jnp.where(used, 1.0 - frac, 0.0), (16, width)).astype(BF16)
        high = jnp.broadcast_to(jnp.where(used, frac, 0.0), (16, width)).astype(BF16)
        row16 = lax.broadcasted_iota(jnp.int32, (16, width), 0).astype(F32)
        for s in range(WINDOW // 16):
            row = (row16 + 16.0 * s).astype(BF16)
            before = (row16 + (16.0 * s - 1.0)).astype(BF16)
            m_ref[16 * s : 16 * (s + 1), 0:width] = jnp.where(
                row == offset, low, jnp.where(before == offset, high, jnp.zeros_like(low))
            )

    def choose(start, width, m_ref):
        windows = jnp.dot(win_ref[...], m_ref[:, 0:width], preferred_element_type=F32)
        index, number = window_number(start, width)
        number = jnp.broadcast_to(number, (CH, width))
        bits = [(number & (1 << i)) != 0 for i in range(6)]

        def pick(low, level):
            if level == 0:
                return windows[CH * low : CH * (low + 1)]
            near = pick(low, level - 1)
            far = low + (1 << (level - 1))
            if far >= N_WIN:
                return near
            return jnp.where(bits[level - 1], pick(far, level - 1), near)

        return pick(0, 6)

    buffers = (m0, m1)
    make_weights(0, BATCH, m0)
    for step in range(FULL_STEPS):
        if step + 1 < FULL_STEPS:
            make_weights((step + 1) * BATCH, BATCH, buffers[(step + 1) % 2])
        total = choose(step * BATCH, BATCH, buffers[step % 2])
        if step < MAIN_STEPS:
            total = total.astype(BF16)
            for i in range(BATCH // LANES):
                lanes = slice(i * LANES, (i + 1) * LANES)
                out_ref[BATCH // LANES * step + i, 0:CH, :] = total[:, lanes]
        else:
            at = step * BATCH - MAIN_COLS
            tail_ref[:, at : at + BATCH] = total
    rest = FULL_STEPS * BATCH
    make_weights(rest, OWN - rest, m0)
    tail_ref[:, rest - MAIN_COLS :] = choose(rest, OWN - rest, m0)

    left = lane_iota(8) < 64
    for d in range(N_LON):
        at = 2 * TAIL * d
        tile, place = at // LANES, at % LANES
        halves = []
        for h in range(2):
            rows = slice(8 * h, 8 * h + 8)
            here = tail_ref[rows, tile * LANES : (tile + 1) * LANES]
            if place + 2 * TAIL > LANES:
                there = tail_ref[rows, (tile + 1) * LANES : (tile + 2) * LANES]
                here = jnp.where(lane_iota(8) >= place, here, there)
            halves.append(pltpu.roll(here, (64 * h - place) % LANES, 1))
        out_ref[d, CH : CH + 8, :] = jnp.where(left, halves[0], halves[1]).astype(BF16)


def cos_sin(product, length, inverse):
    turns = product - jnp.round(product * inverse) * length
    half = turns * (inverse * math.pi)
    z = half * half
    s = -1.0 / 39916800.0
    for c in (1.0 / 362880.0, -1.0 / 5040.0, 1.0 / 120.0, -1.0 / 6.0, 1.0):
        s = s * z + c
    s = s * half
    c0 = 1.0 / 479001600.0
    for c in (-1.0 / 3628800.0, 1.0 / 40320.0, -1.0 / 720.0, 1.0 / 24.0, -0.5, 1.0):
        c0 = c0 * z + c
    return 1.0 - 2.0 * s * s, 2.0 * s * c0


def rotate(cosine, sine, by_cos, by_sin):
    return cosine * by_cos - sine * by_sin, sine * by_cos + cosine * by_sin


def spectral_kernel(numbers_ref, in_ref, out_ref, x0, x1, w_ref, base_ref, p_ref, y_ref):
    lengths = [numbers_ref[CH + turn : CH + turn + 1, :] for turn in range(2)]
    diffusion = numbers_ref[0:CH, :]
    for near in range(NEAR):
        w_ref[LANES * near + SLOT_ROWS : LANES * (near + 1), :] = jnp.zeros(
            (LANES - SLOT_ROWS, 4 * TRUNC), BF16
        )
    left = lane_iota(8) < 64

    for far in range(FAR):
        rows = slice(CH * far, CH * (far + 1))
        for near in range(NEAR):
            l = far * NEAR + near
            main = in_ref[l, 0:CH, :].astype(F32)
            tail = in_ref[l, CH : CH + 8, :].astype(F32)
            swap = pltpu.roll(main, 64, 1)
            first = [
                jnp.where(left, main[0:8], pltpu.roll(tail, 64, 1)),
                jnp.where(left, main[8:16], tail),
            ]
            second = [
                jnp.where(left, swap[0:8], pltpu.roll(tail, HEAD - TAIL, 1)),
                jnp.where(left, swap[8:16], pltpu.roll(tail, LANES - TAIL, 1)),
            ]
            lanes = slice(LANES * near, LANES * (near + 1))
            x0[rows, lanes] = jnp.concatenate(first, axis=0).astype(BF16)
            x1[rows, lanes] = jnp.concatenate(second, axis=0).astype(BF16)

    first_row = lax.broadcasted_iota(jnp.int32, (8, LANES), 0) == 0
    i48 = lax.broadcasted_iota(jnp.int32, (48, LANES), 0)
    factor = jnp.where(
        i48 < 8,
        N_LON * i48,
        jnp.where(i48 < 24, 8 * N_LON * (i48 - 8), jnp.where(i48 < 40, NEAR * (i48 - 24), i48 - 40)),
    ).astype(F32)

    for turn in range(2):
        length = lengths[turn]
        inverse = 1.0 / length
        x_ref = (x0, x1)[turn]
        for block in range(K_BLOCKS):
            wave_f = (lane_iota(1) + block * LANES).astype(F32)
            base_at = base_ref.at[(turn * K_BLOCKS + block) % 2]
            columns = slice(
                (turn * K_BLOCKS + block) * 2 * LANES, (turn * K_BLOCKS + block + 1) * 2 * LANES
            )
            cosine, sine = cos_sin(factor * wave_f, length, inverse)
            base_at[:, 0:LANES] = cosine
            base_at[:, LANES : 2 * LANES] = sine

            def base(i, base_at=base_at):
                return base_at[i : i + 1, 0:LANES], base_at[i : i + 1, LANES : 2 * LANES]

            low_cos, low_sin = cosine[0:8], sine[0:8]
            for pair in range(SLOT_ROWS // 16):
                strips = [rotate(low_cos, low_sin, *base(8 + 2 * pair + h)) for h in range(2)]
                if pair == SLOT_ROWS // 16 - 1:
                    strips[0] = [jnp.where(first_row, v, 0.0) for v in strips[0]]
                    strips[1] = [jnp.zeros_like(v) for v in strips[1]]
                for near in range(NEAR):
                    turned = strips if near == 0 else [rotate(*st, *base(40 + near)) for st in strips]
                    both = jnp.concatenate(
                        [
                            jnp.concatenate([turned[0][0], turned[1][0]], axis=0),
                            jnp.concatenate([turned[0][1], turned[1][1]], axis=0),
                        ],
                        axis=1,
                    )
                    at = LANES * near + 16 * pair
                    w_ref[at : at + 16, columns] = both.astype(BF16)
            partial = jnp.dot(x_ref[...], w_ref[:, columns], preferred_element_type=F32)
            coeff_cos = jnp.zeros((CH, LANES), F32)
            coeff_sin = jnp.zeros((CH, LANES), F32)
            for far in range(FAR):
                here = partial[CH * far : CH * (far + 1)]
                far_cos, far_sin = base(24 + far)
                coeff_cos += far_cos * here[:, 0:LANES] - far_sin * here[:, LANES:]
                coeff_sin += far_sin * here[:, 0:LANES] + far_cos * here[:, LANES:]
            ratio = wave_f / TRUNC
            weight = jnp.where((wave_f == 0.0) | (2.0 * wave_f == length), 1.0, 2.0)
            weight = jnp.where(2.0 * wave_f <= length, weight, 0.0)
            damping = weight / ((1.0 + diffusion * (ratio * ratio)) * length)
            amp_cos = coeff_cos * damping
            amp_sin = coeff_sin * damping
            for far in range(FAR):
                far_cos, far_sin = base(24 + far)
                part = jnp.concatenate(
                    [
                        amp_cos * far_cos + amp_sin * far_sin,
                        amp_sin * far_cos - amp_cos * far_sin,
                    ],
                    axis=1,
                )
                p_ref[CH * far : CH * (far + 1), columns] = part.astype(BF16)
        half = slice(turn * 2 * TRUNC, (turn + 1) * 2 * TRUNC)
        y_ref[turn] = lax.dot_general(
            p_ref[:, half], w_ref[:, half], (((1,), (1,)), ((), ())), preferred_element_type=F32
        )

    lane = lane_iota(8)
    bounds = [(lane * N_LON).astype(F32) - length for length in lengths]

    for far in range(FAR):
        rows = slice(CH * far, CH * (far + 1))
        for near in range(NEAR):
            l = far * NEAR + near
            lanes = slice(LANES * near, LANES * (near + 1))
            pieces = []
            for turn in range(2):
                inside = bounds[turn] < float(-l)
                here = y_ref[turn, rows, lanes]
                pieces.append([jnp.where(inside, here[0:8], 0.0), jnp.where(inside, here[8:16], 0.0)])
            main = [jnp.where(left, pieces[0][h], pltpu.roll(pieces[1][h], 64, 1)) for h in range(2)]
            out_ref[l, 0:CH, :] = jnp.concatenate(main, axis=0).astype(BF16)
            tail = jnp.where(
                lane < TAIL,
                pltpu.roll(pieces[0][0], 64, 1),
                jnp.where(
                    lane < 64,
                    pltpu.roll(pieces[1][0], 64 + TAIL, 1),
                    jnp.where(lane < 64 + TAIL, pieces[0][1], pltpu.roll(pieces[1][1], TAIL, 1)),
                ),
            )
            out_ref[l, CH : CH + 8, :] = tail.astype(BF16)


def final_kernel(in_ref, out_hbm, out_ref, sems):
    part_tiles = OWN // LANES // OUT_PARTS

    def part_copy(part):
        columns = slice(part * part_tiles * LANES, (part + 1) * part_tiles * LANES)
        return pltpu.make_async_copy(out_ref.at[:, columns], out_hbm.at[:, columns], sems.at[part])

    lane = lane_iota(CH).astype(F32).astype(BF16)
    tiles = {}

    def place(source, source_lane, begin, width):
        tile, lane_at = begin // LANES, begin % LANES
        moved = pltpu.roll(source, (lane_at - source_lane) % LANES, 1)
        if tile in tiles:
            tiles[tile] = jnp.where(lane >= lane_at, moved, tiles[tile])
        else:
            tiles[tile] = moved
        if lane_at + width >= LANES:
            out_ref[:, tile * LANES : (tile + 1) * LANES] = tiles.pop(tile)
            if (tile + 1) % part_tiles == 0:
                part_copy(tile // part_tiles).start()
            if lane_at + width > LANES:
                tiles[tile + 1] = moved

    for d in range(N_LON):
        main = in_ref[d, 0:CH, :]
        tail = in_ref[d, CH : CH + 8, :].astype(F32)
        tail = jnp.concatenate([tail, pltpu.roll(tail, 64, 1)], axis=0).astype(BF16)
        for turn in range(2):
            begin = SLOTS * (2 * d + turn)
            place(main, HEAD * turn, begin, HEAD)
            place(tail, TAIL * turn, begin + HEAD, TAIL)
    for part in range(OUT_PARTS):
        part_copy(part).wait()


def vmem():
    return pl.BlockSpec(memory_space=pltpu.VMEM)


def smem():
    return pl.BlockSpec(memory_space=pltpu.SMEM)


def shape(dims, dtype=BF16):
    return pltpu.VMEM(dims, dtype)


def near(x):
    return pltpu.with_memory_space_constraint(x, pltpu.VMEM)


def exchange(blocks):
    return lax.all_to_all(blocks, "lon", split_axis=0, concat_axis=0, tiled=True)


def on_device(field, dep_frac, dep_index, send_list, send_count, cycle_len, diffusion):
    lon_index = lax.axis_index("lon")
    bands = lax.axis_size("lat")
    outward, inward, field_near, index_near, frac_near, len_near, numbers = pl.pallas_call(
        pick_kernel,
        out_shape=(
            shape((CH, HALO)),
            shape((CH, HALO)),
            shape((CH, OWN)),
            shape((2, OWN), jnp.int32),
            shape((OWN // LANES, LANES), F32),
            shape((1, CYCLES), jnp.int32),
            shape((CH + 8, LANES), F32),
        ),
        in_specs=[smem()] * 4 + [vmem()] * 4,
        out_specs=(vmem(),) * 7,
        name="pick_blocks",
    )(
        send_list,
        send_count,
        cycle_len,
        diffusion,
        cycle_len,
        field,
        dep_index,
        dep_frac.reshape(OWN // LANES, LANES),
    )
    pairs = [(i, i + 1) for i in range(1, bands - 1, 2)]
    from_outer = lax.ppermute(outward, "lat", pairs + [(j, i) for i, j in pairs])
    pairs = [(i, i + 1) for i in range(0, bands - 1, 2)]
    from_inner = lax.ppermute(inward, "lat", pairs + [(j, i) for i, j in pairs])

    windows, stencil = pl.pallas_call(
        prepare_kernel,
        out_shape=(shape((CH * OWN_WIN, WINDOW)), shape((2, OWN), F32)),
        in_specs=[vmem(), vmem(), vmem(), vmem()],
        out_specs=(vmem(), vmem()),
        scratch_shapes=[
            pltpu.VMEM((CH, OWN + LANES), BF16),
            pltpu.VMEM((8, OWN + LANES), F32),
        ],
        name="prepare",
    )(near(len_near), near(field_near), near(index_near), near(frac_near))

    departed = pl.pallas_call(
        gather_kernel,
        out_shape=shape((N_LON, CH + 8, LANES)),
        in_specs=[vmem(), vmem(), vmem(), vmem()],
        out_specs=vmem(),
        scratch_shapes=[
            pltpu.VMEM((CH, RIM), BF16),
            pltpu.VMEM((CH * N_WIN, WINDOW), BF16),
            pltpu.VMEM((WINDOW, BATCH), BF16),
            pltpu.VMEM((WINDOW, BATCH), BF16),
            pltpu.VMEM((CH, OWN - MAIN_COLS), F32),
        ],
        name="departure_gather",
    )(near(windows), near(from_outer), near(from_inner), near(stencil))

    received = exchange(departed)

    filtered = pl.pallas_call(
        spectral_kernel,
        out_shape=shape((N_LON, CH + 8, LANES)),
        in_specs=[vmem(), vmem()],
        out_specs=vmem(),
        scratch_shapes=[
            pltpu.VMEM((FAR * CH, NEAR * LANES), BF16),
            pltpu.VMEM((FAR * CH, NEAR * LANES), BF16),
            pltpu.VMEM((NEAR * LANES, 4 * TRUNC), BF16),
            pltpu.VMEM((2, 48, 2 * LANES), F32),
            pltpu.VMEM((FAR * CH, 4 * TRUNC), BF16),
            pltpu.VMEM((2, FAR * CH, NEAR * LANES), F32),
        ],
        name="zonal_filter",
    )(near(numbers), near(received))

    landed = exchange(filtered)

    return pl.pallas_call(
        final_kernel,
        out_shape=jax.ShapeDtypeStruct((CH, OWN), BF16),
        in_specs=[vmem()],
        out_specs=pl.BlockSpec(memory_space=pl.ANY),
        scratch_shapes=[pltpu.VMEM((CH, OWN), BF16), pltpu.SemaphoreType.DMA((OUT_PARTS,))],
        name="unpack_columns",
    )(near(landed))


def solution(mesh):
    placed = (
        P(None, ("lat", "lon")),
        P(("lat", "lon")),
        P(None, ("lat", "lon")),
        P(("lat", "lon"), None, None),
        P(("lat", "lon"), None),
        P("lat", None),
        P(),
    )
    return jax.shard_map(
        on_device, mesh=mesh, in_specs=placed, out_specs=P(None, ("lat", "lon")), check_vma=False
    )
```

```python
import math

import jax
import jax.numpy as jnp
from jax import lax
from jax.experimental import pallas as pl
from jax.experimental.pallas import tpu as pltpu
from jax.sharding import PartitionSpec as P

TRUNC = 640
HALO_BLOCKS = 8
CH = 16
CYCLES = 128
SLOTS = 81
N_LON = 64
OWN = CYCLES * SLOTS
HALO = HALO_BLOCKS * SLOTS
LANES = 128
STRIDE = 255
WINDOW = 256
EXT = OWN + 2 * HALO
N_WIN = (EXT - 2) // STRIDE + 1
HEAD = 64
TAIL = SLOTS - HEAD
SLOT_ROWS = 96
MAIN_COLS = N_LON * LANES
K_BLOCKS = TRUNC // LANES
OWN_WIN = OWN // STRIDE + 1
RIM_OWN = OWN - STRIDE * (OWN_WIN - 1)
RIM = -(-(STRIDE * (N_WIN - OWN_WIN) + WINDOW) // LANES) * LANES
BATCH = 2 * WINDOW
MAIN_STEPS = MAIN_COLS // BATCH
FULL_STEPS = OWN // BATCH
OUT_PARTS = 9
NEAR = 4
FAR = N_LON // NEAR
F32 = jnp.float32
BF16 = jnp.bfloat16


def lane_iota(rows, cols=LANES):
    return lax.broadcasted_iota(jnp.int32, (rows, cols), 1)


def slots_used(length, lon_index):
    return (length - lon_index + (N_LON - 1)) >> 6


def pick_kernel(
    list_ref, count_ref, len_ref, diff_ref, len_row, field_ref, index_ref, frac_ref,
    first_ref, second_ref, field_out, index_out, frac_out, len_out, numbers_ref,
):
    len_out[...] = len_row[...]
    field_out[...] = field_ref[...]
    index_out[...] = index_ref[...]
    frac_out[...] = frac_ref[...]
    lon_index = lax.axis_index("lon")
    lane = lane_iota(CH, 2 * LANES)
    for turn in range(2):
        length = jnp.full((1, LANES), len_ref[0, 2 * lon_index + turn], jnp.int32)
        numbers_ref[CH + turn : CH + turn + 1, :] = length.astype(F32)
    for c in range(CH):
        numbers_ref[c : c + 1, :] = jnp.full((1, LANES), diff_ref[c], F32)
    parity = lax.axis_index("lat") & 1
    for way, out_ref in ((parity, first_ref), (1 - parity, second_ref)):
        blocks = [jnp.zeros((CH, LANES), F32) for _ in range(7)]
        for k in range(HALO_BLOCKS):
            row = jnp.clip(list_ref[0, way, k], 0, CYCLES - 1)
            start = row * SLOTS
            base = jnp.minimum(start >> 7, OWN // LANES - 2)
            shift = start - base * LANES
            place = (SLOTS * k) % LANES
            block = (SLOTS * k) // LANES
            window = field_ref[:, pl.ds(pl.multiple_of(base * LANES, LANES), 2 * LANES)]
            moved = pltpu.roll(window.astype(F32), (place - shift + 2 * LANES) & 255, 1)
            used = jnp.where(k < count_ref[0, way], slots_used(len_ref[0, row], lon_index), 0)
            keep = (lane >= place) & (lane < place + used)
            for half in range(2):
                part = slice(half * LANES, (half + 1) * LANES)
                blocks[block + half] = jnp.where(keep[:, part], moved[:, part], blocks[block + half])
        for i in range(5):
            out_ref[:, i * LANES : (i + 1) * LANES] = blocks[i].astype(BF16)
        out_ref[:, 5 * LANES : HALO] = blocks[5][:, : HALO - 5 * LANES].astype(BF16)


def prepare_kernel(len_ref, field_ref, index_ref, frac_ref, win_ref, where_ref, ext_ref, pair_ref):
    all_used = slots_used(len_ref[...], lax.axis_index("lon"))
    used_slots = [jnp.broadcast_to(all_used[:, r : r + 1], (8, LANES)) for r in range(CYCLES)]
    pair_ref[:, OWN:] = jnp.zeros((8, LANES), F32)
    pair_ref[0:1, 0:OWN] = index_ref[0:1, :].astype(F32)
    for b in range(OWN // LANES):
        pair_ref[1:2, b * LANES : (b + 1) * LANES] = frac_ref[b : b + 1, :]
    lane = lane_iota(8)
    tile = None
    for d in range(N_LON):
        used = used_slots[2 * d : 2 * d + 2]
        begin = 2 * SLOTS * d
        here = jnp.where(
            lane < HEAD,
            pair_ref[:, begin : begin + LANES],
            pair_ref[:, begin + TAIL : begin + TAIL + LANES],
        )
        limit = jnp.where(lane < HEAD, used[0], used[1] + HEAD)
        here = jnp.where(lane < limit, here, -1.0)
        where_ref[:, LANES * d : LANES * (d + 1)] = here[0:2]
        for turn in range(2):
            at = TAIL * (2 * d + turn)
            number, place = at // LANES, at % LANES
            source = begin + SLOTS * turn + HEAD - place
            limit = place + used[turn] - HEAD
            here = jnp.where(lane < limit, pair_ref[:, source : source + LANES], -1.0)
            tile = here if tile is None else jnp.where(lane >= place, here, tile)
            if place + TAIL >= LANES:
                column = MAIN_COLS + LANES * number
                where_ref[:, column : column + LANES] = tile[0:2]
                tile = None
                if place + TAIL > LANES:
                    source += LANES
                    tile = jnp.where(lane < limit - LANES, pair_ref[:, source : source + LANES], -1.0)

    for b in range(OWN // LANES):
        first = (LANES * b) // SLOTS
        last = (LANES * b + LANES - 1) // SLOTS
        limit = used_slots[last] + (SLOTS * last - LANES * b)
        for r in range(last - 1, first - 1, -1):
            here = used_slots[r] + (SLOTS * r - LANES * b)
            limit = jnp.where(lane < SLOTS * (r + 1) - LANES * b, here, limit)
        keep = jnp.where(lane < limit, 1.0, 0.0)
        keep = jnp.concatenate([keep, keep], axis=0).astype(BF16)
        part = slice(b * LANES, (b + 1) * LANES)
        ext_ref[:, part] = field_ref[:, part] * keep
    ext_ref[:, OWN : OWN + LANES] = jnp.zeros((CH, LANES), BF16)
    for q in range(OWN_WIN):
        win_ref[CH * q : CH * (q + 1), :] = ext_ref[:, STRIDE * q : STRIDE * q + WINDOW]


def gather_kernel(own_ref, outer_ref, inner_ref, where_ref, out_ref, rim_ref, win_ref, m0, m1, tail_ref):
    rim_ref[:, RIM_OWN + 2 * HALO :] = jnp.zeros((CH, RIM - RIM_OWN - 2 * HALO), BF16)
    rim_ref[:, 0:RIM_OWN] = own_ref[CH * (OWN_WIN - 1) : CH * OWN_WIN, 0:RIM_OWN]
    even = (lax.axis_index("lat") & 1) == 0

    @pl.when(even)
    def _():
        rim_ref[:, RIM_OWN : RIM_OWN + HALO] = outer_ref[...]
        rim_ref[:, RIM_OWN + HALO : RIM_OWN + 2 * HALO] = inner_ref[...]

    @pl.when(jnp.logical_not(even))
    def _():
        rim_ref[:, RIM_OWN : RIM_OWN + HALO] = inner_ref[...]
        rim_ref[:, RIM_OWN + HALO : RIM_OWN + 2 * HALO] = outer_ref[...]

    win_ref[0 : CH * (OWN_WIN - 1), :] = own_ref[0 : CH * (OWN_WIN - 1), :]
    for q in range(OWN_WIN - 1, N_WIN):
        at = STRIDE * (q - OWN_WIN + 1)
        win_ref[CH * q : CH * (q + 1), :] = rim_ref[:, at : at + WINDOW]

    def window_number(start, width):
        index = where_ref[0:1, pl.ds(start, width)].astype(jnp.int32)
        return index, (index * 32897) >> 23

    def make_weights(start, width, m_ref):
        index, number = window_number(start, width)
        frac = where_ref[1:2, pl.ds(start, width)]
        used = index >= 0
        offset = (index - STRIDE * number).astype(F32)
        offset = jnp.broadcast_to(offset, (16, width)).astype(BF16)
        low = jnp.broadcast_to(jnp.where(used, 1.0 - frac, 0.0), (16, width)).astype(BF16)
        high = jnp.broadcast_to(jnp.where(used, frac, 0.0), (16, width)).astype(BF16)
        row16 = lax.broadcasted_iota(jnp.int32, (16, width), 0).astype(F32)
        for s in range(WINDOW // 16):
            row = (row16 + 16.0 * s).astype(BF16)
            before = (row16 + (16.0 * s - 1.0)).astype(BF16)
            m_ref[16 * s : 16 * (s + 1), 0:width] = jnp.where(
                row == offset, low, jnp.where(before == offset, high, jnp.zeros_like(low))
            )

    def choose(start, width, m_ref):
        windows = jnp.dot(win_ref[...], m_ref[:, 0:width], preferred_element_type=F32)
        index, number = window_number(start, width)
        number = jnp.broadcast_to(number, (CH, width))
        bits = [(number & (1 << i)) != 0 for i in range(6)]

        def pick(low, level):
            if level == 0:
                return windows[CH * low : CH * (low + 1)]
            near = pick(low, level - 1)
            far = low + (1 << (level - 1))
            if far >= N_WIN:
                return near
            return jnp.where(bits[level - 1], pick(far, level - 1), near)

        return pick(0, 6)

    buffers = (m0, m1)
    make_weights(0, BATCH, m0)
    for step in range(FULL_STEPS):
        if step + 1 < FULL_STEPS:
            make_weights((step + 1) * BATCH, BATCH, buffers[(step + 1) % 2])
        total = choose(step * BATCH, BATCH, buffers[step % 2])
        if step < MAIN_STEPS:
            total = total.astype(BF16)
            for i in range(BATCH // LANES):
                lanes = slice(i * LANES, (i + 1) * LANES)
                out_ref[BATCH // LANES * step + i, 0:CH, :] = total[:, lanes]
        else:
            at = step * BATCH - MAIN_COLS
            tail_ref[:, at : at + BATCH] = total
    rest = FULL_STEPS * BATCH
    make_weights(rest, OWN - rest, m0)
    tail_ref[:, rest - MAIN_COLS : OWN - MAIN_COLS] = choose(rest, OWN - rest, m0)
    tail_ref[:, OWN - MAIN_COLS :] = jnp.zeros((CH, LANES), F32)

    for d in range(N_LON):
        at = 2 * TAIL * d
        for h in range(2):
            out_ref[d, CH : CH + 8, 64 * h : 64 * (h + 1)] = tail_ref[
                8 * h : 8 * h + 8, at : at + 64
            ].astype(BF16)


def cos_sin(product, length, inverse):
    turns = product - jnp.round(product * inverse) * length
    half = turns * (inverse * math.pi)
    z = half * half
    s = -1.0 / 39916800.0
    for c in (1.0 / 362880.0, -1.0 / 5040.0, 1.0 / 120.0, -1.0 / 6.0, 1.0):
        s = s * z + c
    s = s * half
    c0 = 1.0 / 479001600.0
    for c in (-1.0 / 3628800.0, 1.0 / 40320.0, -1.0 / 720.0, 1.0 / 24.0, -0.5, 1.0):
        c0 = c0 * z + c
    return 1.0 - 2.0 * s * s, 2.0 * s * c0


def rotate(cosine, sine, by_cos, by_sin):
    return cosine * by_cos - sine * by_sin, sine * by_cos + cosine * by_sin


def spectral_kernel(numbers_ref, in_ref, out_ref, x0, x1, w_ref, base_ref, p_ref, y_ref):
    lengths = [numbers_ref[CH + turn : CH + turn + 1, :] for turn in range(2)]
    diffusion = numbers_ref[0:CH, :]
    for near in range(NEAR):
        w_ref[LANES * near + SLOT_ROWS : LANES * (near + 1), :] = jnp.zeros(
            (LANES - SLOT_ROWS, 4 * TRUNC), BF16
        )
    left = lane_iota(8) < 64

    for far in range(FAR):
        rows = slice(CH * far, CH * (far + 1))
        for near in range(NEAR):
            l = far * NEAR + near
            main = in_ref[l, 0:CH, :].astype(F32)
            tail = in_ref[l, CH : CH + 8, :].astype(F32)
            swap = pltpu.roll(main, 64, 1)
            first = [
                jnp.where(left, main[0:8], pltpu.roll(tail, 64, 1)),
                jnp.where(left, main[8:16], tail),
            ]
            second = [
                jnp.where(left, swap[0:8], pltpu.roll(tail, HEAD - TAIL, 1)),
                jnp.where(left, swap[8:16], pltpu.roll(tail, LANES - TAIL, 1)),
            ]
            lanes = slice(LANES * near, LANES * (near + 1))
            x0[rows, lanes] = jnp.concatenate(first, axis=0).astype(BF16)
            x1[rows, lanes] = jnp.concatenate(second, axis=0).astype(BF16)

    first_row = lax.broadcasted_iota(jnp.int32, (8, LANES), 0) == 0
    i48 = lax.broadcasted_iota(jnp.int32, (48, LANES), 0)
    factor = jnp.where(
        i48 < 8,
        N_LON * i48,
        jnp.where(i48 < 24, 8 * N_LON * (i48 - 8), jnp.where(i48 < 40, NEAR * (i48 - 24), i48 - 40)),
    ).astype(F32)

    for turn in range(2):
        length = lengths[turn]
        inverse = 1.0 / length
        x_ref = (x0, x1)[turn]
        for block in range(K_BLOCKS):
            wave_f = (lane_iota(1) + block * LANES).astype(F32)
            base_at = base_ref.at[(turn * K_BLOCKS + block) % 2]
            columns = slice(
                (turn * K_BLOCKS + block) * 2 * LANES, (turn * K_BLOCKS + block + 1) * 2 * LANES
            )
            cosine, sine = cos_sin(factor * wave_f, length, inverse)
            base_at[:, 0:LANES] = cosine
            base_at[:, LANES : 2 * LANES] = sine

            def base(i, base_at=base_at):
                return base_at[i : i + 1, 0:LANES], base_at[i : i + 1, LANES : 2 * LANES]

            low_cos, low_sin = cosine[0:8], sine[0:8]
            for pair in range(SLOT_ROWS // 16):
                strips = [rotate(low_cos, low_sin, *base(8 + 2 * pair + h)) for h in range(2)]
                if pair == SLOT_ROWS // 16 - 1:
                    strips[0] = [jnp.where(first_row, v, 0.0) for v in strips[0]]
                    strips[1] = [jnp.zeros_like(v) for v in strips[1]]
                for near in range(NEAR):
                    turned = strips if near == 0 else [rotate(*st, *base(40 + near)) for st in strips]
                    both = jnp.concatenate(
                        [
                            jnp.concatenate([turned[0][0], turned[1][0]], axis=0),
                            jnp.concatenate([turned[0][1], turned[1][1]], axis=0),
                        ],
                        axis=1,
                    )
                    at = LANES * near + 16 * pair
                    w_ref[at : at + 16, columns] = both.astype(BF16)
            partial = jnp.dot(x_ref[...], w_ref[:, columns], preferred_element_type=F32)
            coeff_cos = jnp.zeros((CH, LANES), F32)
            coeff_sin = jnp.zeros((CH, LANES), F32)
            for far in range(FAR):
                here = partial[CH * far : CH * (far + 1)]
                far_cos, far_sin = base(24 + far)
                coeff_cos += far_cos * here[:, 0:LANES] - far_sin * here[:, LANES:]
                coeff_sin += far_sin * here[:, 0:LANES] + far_cos * here[:, LANES:]
            ratio = wave_f / TRUNC
            weight = jnp.where((wave_f == 0.0) | (2.0 * wave_f == length), 1.0, 2.0)
            weight = jnp.where(2.0 * wave_f <= length, weight, 0.0)
            damping = weight / ((1.0 + diffusion * (ratio * ratio)) * length)
            amp_cos = coeff_cos * damping
            amp_sin = coeff_sin * damping
            for far in range(FAR):
                far_cos, far_sin = base(24 + far)
                part = jnp.concatenate(
                    [
                        amp_cos * far_cos + amp_sin * far_sin,
                        amp_sin * far_cos - amp_cos * far_sin,
                    ],
                    axis=1,
                )
                p_ref[CH * far : CH * (far + 1), columns] = part.astype(BF16)
        half = slice(turn * 2 * TRUNC, (turn + 1) * 2 * TRUNC)
        y_ref[turn] = lax.dot_general(
            p_ref[:, half], w_ref[:, half], (((1,), (1,)), ((), ())), preferred_element_type=F32
        )

    lane = lane_iota(8)
    bounds = [(lane * N_LON).astype(F32) - length for length in lengths]

    for far in range(FAR):
        rows = slice(CH * far, CH * (far + 1))
        for near in range(NEAR):
            l = far * NEAR + near
            lanes = slice(LANES * near, LANES * (near + 1))
            pieces = []
            for turn in range(2):
                inside = bounds[turn] < float(-l)
                here = y_ref[turn, rows, lanes]
                pieces.append([jnp.where(inside, here[0:8], 0.0), jnp.where(inside, here[8:16], 0.0)])
            main = [jnp.where(left, pieces[0][h], pltpu.roll(pieces[1][h], 64, 1)) for h in range(2)]
            out_ref[l, 0:CH, :] = jnp.concatenate(main, axis=0).astype(BF16)
            tail = jnp.where(
                lane < TAIL,
                pltpu.roll(pieces[0][0], 64, 1),
                jnp.where(
                    lane < 64,
                    pltpu.roll(pieces[1][0], 64 + TAIL, 1),
                    jnp.where(lane < 64 + TAIL, pieces[0][1], pltpu.roll(pieces[1][1], TAIL, 1)),
                ),
            )
            out_ref[l, CH : CH + 8, :] = tail.astype(BF16)


def final_kernel(in_ref, out_hbm, out_ref, sems):
    part_tiles = OWN // LANES // OUT_PARTS

    def part_copy(part):
        columns = slice(part * part_tiles * LANES, (part + 1) * part_tiles * LANES)
        return pltpu.make_async_copy(out_ref.at[:, columns], out_hbm.at[:, columns], sems.at[part])

    started = 0
    for d in range(N_LON):
        main = in_ref[d, 0:CH, :]
        tail = in_ref[d, CH : CH + 8, :]
        for turn in range(2):
            begin = SLOTS * (2 * d + turn)
            out_ref[:, begin : begin + HEAD] = main[:, HEAD * turn : HEAD * (turn + 1)]
            for half in range(2):
                lanes = 64 * half + TAIL * turn
                out_ref[8 * half : 8 * half + 8, begin + HEAD : begin + SLOTS] = tail[
                    :, lanes : lanes + TAIL
                ]
        while started < OUT_PARTS and 2 * SLOTS * (d + 1) >= (started + 1) * part_tiles * LANES:
            part_copy(started).start()
            started += 1
    for part in range(OUT_PARTS):
        part_copy(part).wait()


def vmem():
    return pl.BlockSpec(memory_space=pltpu.VMEM)


def smem():
    return pl.BlockSpec(memory_space=pltpu.SMEM)


def shape(dims, dtype=BF16):
    return pltpu.VMEM(dims, dtype)


def near(x):
    return pltpu.with_memory_space_constraint(x, pltpu.VMEM)


def exchange(blocks):
    return lax.all_to_all(blocks, "lon", split_axis=0, concat_axis=0, tiled=True)


def on_device(field, dep_frac, dep_index, send_list, send_count, cycle_len, diffusion):
    lon_index = lax.axis_index("lon")
    bands = lax.axis_size("lat")
    outward, inward, field_near, index_near, frac_near, len_near, numbers = pl.pallas_call(
        pick_kernel,
        out_shape=(
            shape((CH, HALO)),
            shape((CH, HALO)),
            shape((CH, OWN)),
            shape((2, OWN), jnp.int32),
            shape((OWN // LANES, LANES), F32),
            shape((1, CYCLES), jnp.int32),
            shape((CH + 8, LANES), F32),
        ),
        in_specs=[smem()] * 4 + [vmem()] * 4,
        out_specs=(vmem(),) * 7,
        name="pick_blocks",
    )(
        send_list,
        send_count,
        cycle_len,
        diffusion,
        cycle_len,
        field,
        dep_index,
        dep_frac.reshape(OWN // LANES, LANES),
    )
    pairs = [(i, i + 1) for i in range(1, bands - 1, 2)]
    from_outer = lax.ppermute(outward, "lat", pairs + [(j, i) for i, j in pairs])
    pairs = [(i, i + 1) for i in range(0, bands - 1, 2)]
    from_inner = lax.ppermute(inward, "lat", pairs + [(j, i) for i, j in pairs])

    windows, stencil = pl.pallas_call(
        prepare_kernel,
        out_shape=(shape((CH * OWN_WIN, WINDOW)), shape((2, OWN), F32)),
        in_specs=[vmem(), vmem(), vmem(), vmem()],
        out_specs=(vmem(), vmem()),
        scratch_shapes=[
            pltpu.VMEM((CH, OWN + LANES), BF16),
            pltpu.VMEM((8, OWN + LANES), F32),
        ],
        name="prepare",
    )(near(len_near), near(field_near), near(index_near), near(frac_near))

    departed = pl.pallas_call(
        gather_kernel,
        out_shape=shape((N_LON, CH + 8, LANES)),
        in_specs=[vmem(), vmem(), vmem(), vmem()],
        out_specs=vmem(),
        scratch_shapes=[
            pltpu.VMEM((CH, RIM), BF16),
            pltpu.VMEM((CH * N_WIN, WINDOW), BF16),
            pltpu.VMEM((WINDOW, BATCH), BF16),
            pltpu.VMEM((WINDOW, BATCH), BF16),
            pltpu.VMEM((CH, OWN - MAIN_COLS + LANES), F32),
        ],
        name="departure_gather",
    )(near(windows), near(from_outer), near(from_inner), near(stencil))

    received = exchange(departed)

    filtered = pl.pallas_call(
        spectral_kernel,
        out_shape=shape((N_LON, CH + 8, LANES)),
        in_specs=[vmem(), vmem()],
        out_specs=vmem(),
        scratch_shapes=[
            pltpu.VMEM((FAR * CH, NEAR * LANES), BF16),
            pltpu.VMEM((FAR * CH, NEAR * LANES), BF16),
            pltpu.VMEM((NEAR * LANES, 4 * TRUNC), BF16),
            pltpu.VMEM((2, 48, 2 * LANES), F32),
            pltpu.VMEM((FAR * CH, 4 * TRUNC), BF16),
            pltpu.VMEM((2, FAR * CH, NEAR * LANES), F32),
        ],
        name="zonal_filter",
    )(near(numbers), near(received))

    landed = exchange(filtered)

    return pl.pallas_call(
        final_kernel,
        out_shape=jax.ShapeDtypeStruct((CH, OWN), BF16),
        in_specs=[vmem()],
        out_specs=pl.BlockSpec(memory_space=pl.ANY),
        scratch_shapes=[pltpu.VMEM((CH, OWN), BF16), pltpu.SemaphoreType.DMA((OUT_PARTS,))],
        name="unpack_columns",
    )(near(landed))


def solution(mesh):
    placed = (
        P(None, ("lat", "lon")),
        P(("lat", "lon")),
        P(None, ("lat", "lon")),
        P(("lat", "lon"), None, None),
        P(("lat", "lon"), None),
        P("lat", None),
        P(),
    )
    return jax.shard_map(
        on_device, mesh=mesh, in_specs=placed, out_specs=P(None, ("lat", "lon")), check_vma=False
    )
```

```python
import math

import jax
import jax.numpy as jnp
from jax import lax
from jax.experimental import pallas as pl
from jax.experimental.pallas import tpu as pltpu
from jax.sharding import PartitionSpec as P

TRUNC = 640
HALO_BLOCKS = 8
CH = 16
CYCLES = 128
SLOTS = 81
N_LON = 64
OWN = CYCLES * SLOTS
HALO = HALO_BLOCKS * SLOTS
LANES = 128
STRIDE = 255
WINDOW = 256
EXT = OWN + 2 * HALO
N_WIN = (EXT - 2) // STRIDE + 1
HEAD = 64
TAIL = SLOTS - HEAD
SLOT_ROWS = 96
MAIN_COLS = N_LON * LANES
K_BLOCKS = TRUNC // LANES
OWN_WIN = OWN // STRIDE + 1
RIM_OWN = OWN - STRIDE * (OWN_WIN - 1)
RIM = -(-(STRIDE * (N_WIN - OWN_WIN) + WINDOW) // LANES) * LANES
BATCH = 2 * WINDOW
MAIN_STEPS = MAIN_COLS // BATCH
FULL_STEPS = OWN // BATCH
OUT_PARTS = 9
NEAR = 4
FAR = N_LON // NEAR
F32 = jnp.float32
BF16 = jnp.bfloat16


def lane_iota(rows, cols=LANES):
    return lax.broadcasted_iota(jnp.int32, (rows, cols), 1)


def slots_used(length, lon_index):
    return (length - lon_index + (N_LON - 1)) >> 6


def pick_kernel(
    list_ref, count_ref, len_ref, diff_ref, len_row, field_ref, index_ref, frac_ref,
    first_ref, second_ref, field_out, index_out, frac_out, len_out, numbers_ref,
):
    len_out[...] = len_row[...]
    field_out[...] = field_ref[...]
    index_out[...] = index_ref[...]
    frac_out[...] = frac_ref[...]
    lon_index = lax.axis_index("lon")
    lane = lane_iota(CH, 2 * LANES)
    for turn in range(2):
        length = jnp.full((1, LANES), len_ref[0, 2 * lon_index + turn], jnp.int32)
        numbers_ref[CH + turn : CH + turn + 1, :] = length.astype(F32)
    for c in range(CH):
        numbers_ref[c : c + 1, :] = jnp.full((1, LANES), diff_ref[c], F32)
    parity = lax.axis_index("lat") & 1
    for way, out_ref in ((parity, first_ref), (1 - parity, second_ref)):
        blocks = [jnp.zeros((CH, LANES), F32) for _ in range(7)]
        for k in range(HALO_BLOCKS):
            row = jnp.clip(list_ref[0, way, k], 0, CYCLES - 1)
            start = row * SLOTS
            base = jnp.minimum(start >> 7, OWN // LANES - 2)
            shift = start - base * LANES
            place = (SLOTS * k) % LANES
            block = (SLOTS * k) // LANES
            window = field_ref[:, pl.ds(pl.multiple_of(base * LANES, LANES), 2 * LANES)]
            moved = pltpu.roll(window.astype(F32), (place - shift + 2 * LANES) & 255, 1)
            used = jnp.where(k < count_ref[0, way], slots_used(len_ref[0, row], lon_index), 0)
            keep = (lane >= place) & (lane < place + used)
            for half in range(2):
                part = slice(half * LANES, (half + 1) * LANES)
                blocks[block + half] = jnp.where(keep[:, part], moved[:, part], blocks[block + half])
        for i in range(5):
            out_ref[:, i * LANES : (i + 1) * LANES] = blocks[i].astype(BF16)
        out_ref[:, 5 * LANES : HALO] = blocks[5][:, : HALO - 5 * LANES].astype(BF16)


def prepare_kernel(len_ref, field_ref, index_ref, frac_ref, win_ref, where_ref, ext_ref, pair_ref):
    all_used = slots_used(len_ref[...], lax.axis_index("lon"))
    used_slots = [jnp.broadcast_to(all_used[:, r : r + 1], (8, LANES)) for r in range(CYCLES)]
    pair_ref[:, OWN:] = jnp.zeros((8, LANES), F32)
    pair_ref[0:1, 0:OWN] = index_ref[0:1, :].astype(F32)
    for b in range(OWN // LANES):
        pair_ref[1:2, b * LANES : (b + 1) * LANES] = frac_ref[b : b + 1, :]
    lane = lane_iota(8)
    tile = None
    for d in range(N_LON):
        used = used_slots[2 * d : 2 * d + 2]
        begin = 2 * SLOTS * d
        here = jnp.where(
            lane < HEAD,
            pair_ref[:, begin : begin + LANES],
            pair_ref[:, begin + TAIL : begin + TAIL + LANES],
        )
        limit = jnp.where(lane < HEAD, used[0], used[1] + HEAD)
        here = jnp.where(lane < limit, here, -1.0)
        where_ref[:, LANES * d : LANES * (d + 1)] = here[0:2]
        for turn in range(2):
            at = TAIL * (2 * d + turn)
            number, place = at // LANES, at % LANES
            source = begin + SLOTS * turn + HEAD - place
            limit = place + used[turn] - HEAD
            here = jnp.where(lane < limit, pair_ref[:, source : source + LANES], -1.0)
            tile = here if tile is None else jnp.where(lane >= place, here, tile)
            if place + TAIL >= LANES:
                column = MAIN_COLS + LANES * number
                where_ref[:, column : column + LANES] = tile[0:2]
                tile = None
                if place + TAIL > LANES:
                    source += LANES
                    tile = jnp.where(lane < limit - LANES, pair_ref[:, source : source + LANES], -1.0)

    for b in range(OWN // LANES):
        first = (LANES * b) // SLOTS
        last = (LANES * b + LANES - 1) // SLOTS
        limit = used_slots[last] + (SLOTS * last - LANES * b)
        for r in range(last - 1, first - 1, -1):
            here = used_slots[r] + (SLOTS * r - LANES * b)
            limit = jnp.where(lane < SLOTS * (r + 1) - LANES * b, here, limit)
        keep = jnp.where(lane < limit, 1.0, 0.0)
        keep = jnp.concatenate([keep, keep], axis=0).astype(BF16)
        part = slice(b * LANES, (b + 1) * LANES)
        ext_ref[:, part] = field_ref[:, part] * keep
    ext_ref[:, OWN : OWN + LANES] = jnp.zeros((CH, LANES), BF16)
    for q in range(OWN_WIN):
        win_ref[CH * q : CH * (q + 1), :] = ext_ref[:, STRIDE * q : STRIDE * q + WINDOW]


def gather_kernel(own_ref, outer_ref, inner_ref, where_ref, out_ref, rim_ref, win_ref, m0, m1, tail_ref):
    rim_ref[:, RIM_OWN + 2 * HALO :] = jnp.zeros((CH, RIM - RIM_OWN - 2 * HALO), BF16)
    rim_ref[:, 0:RIM_OWN] = own_ref[CH * (OWN_WIN - 1) : CH * OWN_WIN, 0:RIM_OWN]
    even = (lax.axis_index("lat") & 1) == 0

    @pl.when(even)
    def _():
        rim_ref[:, RIM_OWN : RIM_OWN + HALO] = outer_ref[...]
        rim_ref[:, RIM_OWN + HALO : RIM_OWN + 2 * HALO] = inner_ref[...]

    @pl.when(jnp.logical_not(even))
    def _():
        rim_ref[:, RIM_OWN : RIM_OWN + HALO] = inner_ref[...]
        rim_ref[:, RIM_OWN + HALO : RIM_OWN + 2 * HALO] = outer_ref[...]

    win_ref[0 : CH * (OWN_WIN - 1), :] = own_ref[0 : CH * (OWN_WIN - 1), :]
    for q in range(OWN_WIN - 1, N_WIN):
        at = STRIDE * (q - OWN_WIN + 1)
        win_ref[CH * q : CH * (q + 1), :] = rim_ref[:, at : at + WINDOW]

    def window_number(start, width):
        index = where_ref[0:1, pl.ds(start, width)].astype(jnp.int32)
        return index, (index * 32897) >> 23

    def make_weights(start, width, m_ref):
        index, number = window_number(start, width)
        frac = where_ref[1:2, pl.ds(start, width)]
        used = index >= 0
        offset = (index - STRIDE * number).astype(F32)
        offset = jnp.broadcast_to(offset, (16, width)).astype(BF16)
        low = jnp.broadcast_to(jnp.where(used, 1.0 - frac, 0.0), (16, width)).astype(BF16)
        high = jnp.broadcast_to(jnp.where(used, frac, 0.0), (16, width)).astype(BF16)
        row16 = lax.broadcasted_iota(jnp.int32, (16, width), 0).astype(F32)
        for s in range(WINDOW // 16):
            row = (row16 + 16.0 * s).astype(BF16)
            before = (row16 + (16.0 * s - 1.0)).astype(BF16)
            m_ref[16 * s : 16 * (s + 1), 0:width] = jnp.where(
                row == offset, low, jnp.where(before == offset, high, jnp.zeros_like(low))
            )

    def choose(start, width, m_ref):
        windows = jnp.dot(win_ref[...], m_ref[:, 0:width], preferred_element_type=F32)
        index, number = window_number(start, width)
        number = jnp.broadcast_to(number, (CH, width))
        bits = [(number & (1 << i)) != 0 for i in range(6)]

        def pick(low, level):
            if level == 0:
                return windows[CH * low : CH * (low + 1)]
            near = pick(low, level - 1)
            far = low + (1 << (level - 1))
            if far >= N_WIN:
                return near
            return jnp.where(bits[level - 1], pick(far, level - 1), near)

        return pick(0, 6)

    buffers = (m0, m1)
    make_weights(0, BATCH, m0)
    for step in range(FULL_STEPS):
        if step + 1 < FULL_STEPS:
            make_weights((step + 1) * BATCH, BATCH, buffers[(step + 1) % 2])
        total = choose(step * BATCH, BATCH, buffers[step % 2])
        if step < MAIN_STEPS:
            total = total.astype(BF16)
            for i in range(BATCH // LANES):
                lanes = slice(i * LANES, (i + 1) * LANES)
                out_ref[BATCH // LANES * step + i, 0:CH, :] = total[:, lanes]
        else:
            at = step * BATCH - MAIN_COLS
            tail_ref[:, at : at + BATCH] = total
    rest = FULL_STEPS * BATCH
    make_weights(rest, OWN - rest, m0)
    tail_ref[:, rest - MAIN_COLS : OWN - MAIN_COLS] = choose(rest, OWN - rest, m0)
    tail_ref[:, OWN - MAIN_COLS :] = jnp.zeros((CH, LANES), F32)

    for d in range(N_LON):
        at = 2 * TAIL * d
        for h in range(2):
            out_ref[d, CH : CH + 8, 64 * h : 64 * (h + 1)] = tail_ref[
                8 * h : 8 * h + 8, at : at + 64
            ].astype(BF16)


def cos_sin(product, length, inverse):
    turns = product - jnp.round(product * inverse) * length
    half = turns * (inverse * math.pi)
    z = half * half
    s = -1.0 / 39916800.0
    for c in (1.0 / 362880.0, -1.0 / 5040.0, 1.0 / 120.0, -1.0 / 6.0, 1.0):
        s = s * z + c
    s = s * half
    c0 = 1.0 / 479001600.0
    for c in (-1.0 / 3628800.0, 1.0 / 40320.0, -1.0 / 720.0, 1.0 / 24.0, -0.5, 1.0):
        c0 = c0 * z + c
    return 1.0 - 2.0 * s * s, 2.0 * s * c0


def rotate(cosine, sine, by_cos, by_sin):
    return cosine * by_cos - sine * by_sin, sine * by_cos + cosine * by_sin


def spectral_kernel(numbers_ref, in_ref, out_ref, x0, x1, w_ref, base_ref, p_ref, y_ref):
    lengths = [numbers_ref[CH + turn : CH + turn + 1, :] for turn in range(2)]
    diffusion = numbers_ref[0:CH, :]
    for near in range(NEAR):
        w_ref[LANES * near + SLOT_ROWS : LANES * (near + 1), :] = jnp.zeros(
            (LANES - SLOT_ROWS, 4 * TRUNC), BF16
        )
    left = lane_iota(8) < 64
    left_half = lane_iota(CH).astype(F32).astype(BF16) < 64.0

    for far in range(FAR):
        rows = slice(CH * far, CH * (far + 1))
        for near in range(NEAR):
            l = far * NEAR + near
            main = in_ref[l, 0:CH, :]
            tail = in_ref[l, CH : CH + 8, :].astype(F32)
            first = jnp.concatenate([pltpu.roll(tail, 64, 1), tail], axis=0).astype(BF16)
            second = [pltpu.roll(tail, HEAD - TAIL, 1), pltpu.roll(tail, LANES - TAIL, 1)]
            second = jnp.concatenate(second, axis=0).astype(BF16)
            lanes = slice(LANES * near, LANES * (near + 1))
            x0[rows, lanes] = jnp.where(left_half, main, first)
            x1[rows, lanes] = jnp.where(left_half, pltpu.roll(main, 64, 1), second)

    first_row = lax.broadcasted_iota(jnp.int32, (8, LANES), 0) == 0
    i48 = lax.broadcasted_iota(jnp.int32, (48, LANES), 0)
    factor = jnp.where(
        i48 < 8,
        N_LON * i48,
        jnp.where(i48 < 24, 8 * N_LON * (i48 - 8), jnp.where(i48 < 40, NEAR * (i48 - 24), i48 - 40)),
    ).astype(F32)

    for turn in range(2):
        length = lengths[turn]
        inverse = 1.0 / length
        x_ref = (x0, x1)[turn]
        for block in range(K_BLOCKS):
            wave_f = (lane_iota(1) + block * LANES).astype(F32)
            base_at = base_ref.at[(turn * K_BLOCKS + block) % 2]
            columns = slice(
                (turn * K_BLOCKS + block) * 2 * LANES, (turn * K_BLOCKS + block + 1) * 2 * LANES
            )
            cosine, sine = cos_sin(factor * wave_f, length, inverse)
            base_at[:, 0:LANES] = cosine
            base_at[:, LANES : 2 * LANES] = sine

            def base(i, base_at=base_at):
                return base_at[i : i + 1, 0:LANES], base_at[i : i + 1, LANES : 2 * LANES]

            low_cos, low_sin = cosine[0:8], sine[0:8]
            for pair in range(SLOT_ROWS // 16):
                strips = [rotate(low_cos, low_sin, *base(8 + 2 * pair + h)) for h in range(2)]
                if pair == SLOT_ROWS // 16 - 1:
                    strips[0] = [jnp.where(first_row, v, 0.0) for v in strips[0]]
                    strips[1] = [jnp.zeros_like(v) for v in strips[1]]
                for near in range(NEAR):
                    turned = strips if near == 0 else [rotate(*st, *base(40 + near)) for st in strips]
                    both = jnp.concatenate(
                        [
                            jnp.concatenate([turned[0][0], turned[1][0]], axis=0),
                            jnp.concatenate([turned[0][1], turned[1][1]], axis=0),
                        ],
                        axis=1,
                    )
                    at = LANES * near + 16 * pair
                    w_ref[at : at + 16, columns] = both.astype(BF16)
            partial = jnp.dot(x_ref[...], w_ref[:, columns], preferred_element_type=F32)
            coeff_cos = jnp.zeros((CH, LANES), F32)
            coeff_sin = jnp.zeros((CH, LANES), F32)
            for far in range(FAR):
                here = partial[CH * far : CH * (far + 1)]
                far_cos, far_sin = base(24 + far)
                coeff_cos += far_cos * here[:, 0:LANES] - far_sin * here[:, LANES:]
                coeff_sin += far_sin * here[:, 0:LANES] + far_cos * here[:, LANES:]
            ratio = wave_f / TRUNC
            weight = jnp.where((wave_f == 0.0) | (2.0 * wave_f == length), 1.0, 2.0)
            weight = jnp.where(2.0 * wave_f <= length, weight, 0.0)
            damping = weight / ((1.0 + diffusion * (ratio * ratio)) * length)
            amp_cos = coeff_cos * damping
            amp_sin = coeff_sin * damping
            for far in range(FAR):
                far_cos, far_sin = base(24 + far)
                part = jnp.concatenate(
                    [
                        amp_cos * far_cos + amp_sin * far_sin,
                        amp_sin * far_cos - amp_cos * far_sin,
                    ],
                    axis=1,
                )
                p_ref[CH * far : CH * (far + 1), columns] = part.astype(BF16)
        half = slice(turn * 2 * TRUNC, (turn + 1) * 2 * TRUNC)
        y_ref[turn] = lax.dot_general(
            p_ref[:, half], w_ref[:, half], (((1,), (1,)), ((), ())), preferred_element_type=F32
        )

    lane = lane_iota(8)
    bounds = [(lane * N_LON).astype(F32) - length for length in lengths]

    for far in range(FAR):
        rows = slice(CH * far, CH * (far + 1))
        for near in range(NEAR):
            l = far * NEAR + near
            lanes = slice(LANES * near, LANES * (near + 1))
            pieces = []
            for turn in range(2):
                inside = bounds[turn] < float(-l)
                here = y_ref[turn, rows, lanes]
                pieces.append([jnp.where(inside, here[0:8], 0.0), jnp.where(inside, here[8:16], 0.0)])
            main = [jnp.where(left, pieces[0][h], pltpu.roll(pieces[1][h], 64, 1)) for h in range(2)]
            out_ref[l, 0:CH, :] = jnp.concatenate(main, axis=0).astype(BF16)
            tail = jnp.where(
                lane < TAIL,
                pltpu.roll(pieces[0][0], 64, 1),
                jnp.where(
                    lane < 64,
                    pltpu.roll(pieces[1][0], 64 + TAIL, 1),
                    jnp.where(lane < 64 + TAIL, pieces[0][1], pltpu.roll(pieces[1][1], TAIL, 1)),
                ),
            )
            out_ref[l, CH : CH + 8, :] = tail.astype(BF16)


def final_kernel(in_ref, out_hbm, out_ref, sems):
    part_tiles = OWN // LANES // OUT_PARTS

    def part_copy(part):
        columns = slice(part * part_tiles * LANES, (part + 1) * part_tiles * LANES)
        return pltpu.make_async_copy(out_ref.at[:, columns], out_hbm.at[:, columns], sems.at[part])

    started = 0
    for d in range(N_LON):
        main = in_ref[d, 0:CH, :]
        tail = in_ref[d, CH : CH + 8, :]
        for turn in range(2):
            begin = SLOTS * (2 * d + turn)
            out_ref[:, begin : begin + HEAD] = main[:, HEAD * turn : HEAD * (turn + 1)]
            for half in range(2):
                lanes = 64 * half + TAIL * turn
                out_ref[8 * half : 8 * half + 8, begin + HEAD : begin + SLOTS] = tail[
                    :, lanes : lanes + TAIL
                ]
        while started < OUT_PARTS and 2 * SLOTS * (d + 1) >= (started + 1) * part_tiles * LANES:
            part_copy(started).start()
            started += 1
    for part in range(OUT_PARTS):
        part_copy(part).wait()


def vmem():
    return pl.BlockSpec(memory_space=pltpu.VMEM)


def smem():
    return pl.BlockSpec(memory_space=pltpu.SMEM)


def shape(dims, dtype=BF16):
    return pltpu.VMEM(dims, dtype)


def near(x):
    return pltpu.with_memory_space_constraint(x, pltpu.VMEM)


def exchange(blocks):
    return lax.all_to_all(blocks, "lon", split_axis=0, concat_axis=0, tiled=True)


def on_device(field, dep_frac, dep_index, send_list, send_count, cycle_len, diffusion):
    lon_index = lax.axis_index("lon")
    bands = lax.axis_size("lat")
    outward, inward, field_near, index_near, frac_near, len_near, numbers = pl.pallas_call(
        pick_kernel,
        out_shape=(
            shape((CH, HALO)),
            shape((CH, HALO)),
            shape((CH, OWN)),
            shape((2, OWN), jnp.int32),
            shape((OWN // LANES, LANES), F32),
            shape((1, CYCLES), jnp.int32),
            shape((CH + 8, LANES), F32),
        ),
        in_specs=[smem()] * 4 + [vmem()] * 4,
        out_specs=(vmem(),) * 7,
        name="pick_blocks",
    )(
        send_list,
        send_count,
        cycle_len,
        diffusion,
        cycle_len,
        field,
        dep_index,
        dep_frac.reshape(OWN // LANES, LANES),
    )
    pairs = [(i, i + 1) for i in range(1, bands - 1, 2)]
    from_outer = lax.ppermute(outward, "lat", pairs + [(j, i) for i, j in pairs])
    pairs = [(i, i + 1) for i in range(0, bands - 1, 2)]
    from_inner = lax.ppermute(inward, "lat", pairs + [(j, i) for i, j in pairs])

    windows, stencil = pl.pallas_call(
        prepare_kernel,
        out_shape=(shape((CH * OWN_WIN, WINDOW)), shape((2, OWN), F32)),
        in_specs=[vmem(), vmem(), vmem(), vmem()],
        out_specs=(vmem(), vmem()),
        scratch_shapes=[
            pltpu.VMEM((CH, OWN + LANES), BF16),
            pltpu.VMEM((8, OWN + LANES), F32),
        ],
        name="prepare",
    )(near(len_near), near(field_near), near(index_near), near(frac_near))

    departed = pl.pallas_call(
        gather_kernel,
        out_shape=shape((N_LON, CH + 8, LANES)),
        in_specs=[vmem(), vmem(), vmem(), vmem()],
        out_specs=vmem(),
        scratch_shapes=[
            pltpu.VMEM((CH, RIM), BF16),
            pltpu.VMEM((CH * N_WIN, WINDOW), BF16),
            pltpu.VMEM((WINDOW, BATCH), BF16),
            pltpu.VMEM((WINDOW, BATCH), BF16),
            pltpu.VMEM((CH, OWN - MAIN_COLS + LANES), F32),
        ],
        name="departure_gather",
    )(near(windows), near(from_outer), near(from_inner), near(stencil))

    received = exchange(departed)

    filtered = pl.pallas_call(
        spectral_kernel,
        out_shape=shape((N_LON, CH + 8, LANES)),
        in_specs=[vmem(), vmem()],
        out_specs=vmem(),
        scratch_shapes=[
            pltpu.VMEM((FAR * CH, NEAR * LANES), BF16),
            pltpu.VMEM((FAR * CH, NEAR * LANES), BF16),
            pltpu.VMEM((NEAR * LANES, 4 * TRUNC), BF16),
            pltpu.VMEM((2, 48, 2 * LANES), F32),
            pltpu.VMEM((FAR * CH, 4 * TRUNC), BF16),
            pltpu.VMEM((2, FAR * CH, NEAR * LANES), F32),
        ],
        name="zonal_filter",
    )(near(numbers), near(received))

    landed = exchange(filtered)

    return pl.pallas_call(
        final_kernel,
        out_shape=jax.ShapeDtypeStruct((CH, OWN), BF16),
        in_specs=[vmem()],
        out_specs=pl.BlockSpec(memory_space=pl.ANY),
        scratch_shapes=[pltpu.VMEM((CH, OWN), BF16), pltpu.SemaphoreType.DMA((OUT_PARTS,))],
        name="unpack_columns",
    )(near(landed))


def solution(mesh):
    placed = (
        P(None, ("lat", "lon")),
        P(("lat", "lon")),
        P(None, ("lat", "lon")),
        P(("lat", "lon"), None, None),
        P(("lat", "lon"), None),
        P("lat", None),
        P(),
    )
    return jax.shard_map(
        on_device, mesh=mesh, in_specs=placed, out_specs=P(None, ("lat", "lon")), check_vma=False
    )
```
